32 devices in a mesh: grp: 2 (over y), col: 4 (over z), seq: 4 (over x, core).
Axes of the slice: x: 2, y: 2, z: 4, core: 2. Of those that a mesh axis runs over, the one named last changes fastest.
Arguments:
- row_query: bfloat16 [256, 16, 768], P(('grp', 'seq'), 'col'), parts along dimension 0, may hold values from -6 to 6
- row_key: bfloat16 [256, 16, 768], P(('grp', 'seq'), 'col'), parts along dimension 0, may hold values from -6 to 6
- row_value: bfloat16 [256, 16, 768], P(('grp', 'seq'), 'col'), parts along dimension 0, may hold values from -6 to 6
- row_grad: bfloat16 [256, 16, 768], P(('grp', 'seq'), 'col'), parts along dimension 0, may hold values from -48 to 48
- col_query: bfloat16 [256, 16, 768], P(('grp', 'seq'), 'col'), parts along dimension 0, may hold values from -11 to 11
- col_key: bfloat16 [256, 16, 768], P(('grp', 'seq'), 'col'), parts along dimension 0, may hold values from -11 to 11
- col_value: bfloat16 [256, 16, 768], P(('grp', 'seq'), 'col'), parts along dimension 0, may hold values from -6 to 6
- col_grad: bfloat16 [256, 16, 768], P(('grp', 'seq'), 'col'), parts along dimension 0, may hold values from -48 to 48
Outputs:
- row_dquery: bfloat16 [256, 16, 768], P(('grp', 'seq'), 'col'), parts along dimension 0
- row_dkey: bfloat16 [256, 16, 768], P(('grp', 'seq'), 'col'), parts along dimension 0
- row_dvalue: bfloat16 [256, 16, 768], P(('grp', 'seq'), 'col'), parts along dimension 0
- col_dquery: bfloat16 [256, 16, 768], P(('grp', 'seq'), 'col'), parts along dimension 0
- col_dkey: bfloat16 [256, 16, 768], P(('grp', 'seq'), 'col'), parts along dimension 0
- col_dvalue: bfloat16 [256, 16, 768], P(('grp', 'seq'), 'col'), parts along dimension 0
The draws below stay inside these ranges and needn't reach their ends.
There are 2 independent parts, one for each index of `grp`. The reference program is written for one: setup_inputs(seed, part) draws one part's arguments, and reference() takes and returns one part's arrays. A program takes and returns all parts, laid end to end along the dimension named above; each array names one. Nothing has to cross between parts.
All inputs are finite; a program needn't handle non-finite values.
Results may differ from the reference program's by a relative error of at most 0.009.
Values may be sent and summed in bfloat16 or wider, within the bound.
No kernel may reach another device: no remote copies, remote signals or barrier semaphores. Data moves between devices by JAX's collectives and lax.ppermute only.
A program may use at most 64 MiB of HBM per device.

```python
import jax
import jax.numpy as jnp
from jax import lax

HEADS = 12
HEAD = 64
WIDTH = 768
SEQS = 128
COLS = 16


def row_pair(key):
    key_query, key_keys = jax.random.split(key, 2)
    shape = (SEQS, COLS, WIDTH)
    query_row_block = jnp.clip(jax.random.normal(key_query, shape, jnp.float32), -6.0, 6.0)
    key_row_block = jnp.clip(jax.random.normal(key_keys, shape, jnp.float32), -6.0, 6.0)
    return (query_row_block, key_row_block)


def column_pair(key):
    key_query, key_keys = jax.random.split(key, 2)
    shape = (SEQS, COLS, WIDTH)
    query_row_block = jnp.clip(jax.random.normal(key_query, shape, jnp.float32), -11.0, 11.0)
    key_row_block = jnp.clip(jax.random.normal(key_keys, shape, jnp.float32), -11.0, 11.0)
    return (query_row_block, key_row_block)


def draw_row_query(key, part):
    return row_pair(jax.random.fold_in(key, 101))[0].astype(jnp.bfloat16)


def draw_row_key(key, part):
    return row_pair(jax.random.fold_in(key, 101))[1].astype(jnp.bfloat16)


def draw_col_query(key, part):
    return column_pair(jax.random.fold_in(key, 202))[0].astype(jnp.bfloat16)


def draw_col_key(key, part):
    return column_pair(jax.random.fold_in(key, 202))[1].astype(jnp.bfloat16)


def levels(rng, extent, cuts, smallest, top_value):
    gain = 1.0
    for dim, shards_of in cuts:
        steps = jax.random.uniform(jax.random.fold_in(jax.random.fold_in(rng, 6), dim), (shards_of,), jnp.float32, smallest / len(cuts), top_value / len(cuts))
        gain = gain * jnp.repeat(jnp.exp(steps), extent[dim] // shards_of).reshape((-1,) + (1,) * (len(extent) - 1 - dim))
    return gain


def scatter_about(own_key, extent, scale, bound, cuts=(), kind=jnp.bfloat16):
    values = scale * jax.random.normal(own_key, extent, jnp.float32)
    if cuts:
        values = values * levels(own_key, extent, cuts, -0.22, 0.18)
    return jnp.clip(values, -bound, bound).astype(kind)


def setup_inputs(seed: int = 0, part: int = 0) -> dict:
    streams_of = jax.random.split(jax.random.key(seed), 9)
    own_keys = jax.random.split(jax.random.fold_in(streams_of[8], part), 9)
    row_query = draw_row_query(jax.random.fold_in(jax.random.fold_in(streams_of[8], part), 71), part)
    row_key = draw_row_key(jax.random.fold_in(jax.random.fold_in(streams_of[8], part), 71), part)
    row_value = scatter_about(own_keys[2], (SEQS, COLS, WIDTH), 1.0, 6.0, ((0, 4), (1, 4)))
    row_grad = scatter_about(own_keys[3], (SEQS, COLS, WIDTH), 8.0, 48.0, ((0, 4), (1, 4)))
    col_query = draw_col_query(jax.random.fold_in(jax.random.fold_in(streams_of[8], part), 71), part)
    col_key = draw_col_key(jax.random.fold_in(jax.random.fold_in(streams_of[8], part), 71), part)
    col_value = scatter_about(own_keys[6], (SEQS, COLS, WIDTH), 1.0, 6.0, ((0, 4), (1, 4)))
    col_grad = scatter_about(own_keys[7], (SEQS, COLS, WIDTH), 8.0, 48.0, ((0, 4), (1, 4)))
    return dict(row_query=row_query, row_key=row_key, row_value=row_value, row_grad=row_grad, col_query=col_query, col_key=col_key, col_value=col_value, col_grad=col_grad)


def heads_of(block):
    return block.astype(jnp.float32).reshape(block.shape[0], block.shape[1], HEADS, HEAD)


def lowered(values):
    return lax.optimization_barrier(values.astype(jnp.bfloat16)).astype(jnp.float32)


def column_one(items):
    col_scale = HEAD ** -0.5
    query_row_block = items[0].astype(jnp.float32).reshape(SEQS, HEADS, HEAD)
    key_row_block = items[1].astype(jnp.float32).reshape(SEQS, HEADS, HEAD)
    value_row_block = items[2].astype(jnp.float32).reshape(SEQS, HEADS, HEAD)
    gradient_row_block = items[3].astype(jnp.float32).reshape(SEQS, HEADS, HEAD)
    scores = jnp.einsum("she,the->hst", query_row_block, key_row_block) * col_scale
    prob_grad = jnp.einsum("she,the->hst", gradient_row_block, value_row_block)
    col_probs = jax.nn.softmax(scores, axis=-1)
    attention_weight_rows = lowered(col_probs)
    col_delta = jnp.sum(col_probs * prob_grad, axis=-1, keepdims=True)
    score_gradient_part = lowered(col_probs * (prob_grad - col_delta) * col_scale)
    query_grad = jnp.einsum("hst,the->she", score_gradient_part, key_row_block)
    key_gradient_part = jnp.einsum("hst,she->the", score_gradient_part, query_row_block)
    value_gradient_part = jnp.einsum("hst,she->the", attention_weight_rows, gradient_row_block)
    return (query_grad.astype(jnp.bfloat16).reshape(SEQS, WIDTH),
            key_gradient_part.astype(jnp.bfloat16).reshape(SEQS, WIDTH),
            value_gradient_part.astype(jnp.bfloat16).reshape(SEQS, WIDTH))


def reference(row_query, row_key, row_value, row_grad, col_query, col_key, col_value, col_grad):
    row_scale = (HEAD ** -0.5) * (SEQS ** -0.5)
    query_row_block = heads_of(row_query)
    key_row_block = heads_of(row_key)
    value_row_block = heads_of(row_value)
    gradient_row_block = heads_of(row_grad)
    scores = jnp.einsum("sihe,sjhe->hij", query_row_block, key_row_block) * row_scale
    prob_grad = jnp.einsum("sihe,sjhe->hij", gradient_row_block, value_row_block)
    row_probs = jax.nn.softmax(scores, axis=-1)
    attention_weight_rows = lowered(row_probs)
    row_delta = jnp.sum(row_probs * prob_grad, axis=-1, keepdims=True)
    score_gradient_part = lowered(row_probs * (prob_grad - row_delta) * row_scale)
    row_dquery = jnp.einsum("hij,sjhe->sihe", score_gradient_part, key_row_block).astype(jnp.bfloat16).reshape(SEQS, COLS, WIDTH)
    row_dkey = jnp.einsum("hij,sihe->sjhe", score_gradient_part, query_row_block).astype(jnp.bfloat16).reshape(SEQS, COLS, WIDTH)
    row_dvalue = jnp.einsum("hij,sihe->sjhe", attention_weight_rows, gradient_row_block).astype(jnp.bfloat16).reshape(SEQS, COLS, WIDTH)
    results = lax.map(column_one, (jnp.transpose(col_query, (1, 0, 2)), jnp.transpose(col_key, (1, 0, 2)),
                                   jnp.transpose(col_value, (1, 0, 2)), jnp.transpose(col_grad, (1, 0, 2))))
    col_dquery = jnp.transpose(results[0], (1, 0, 2))
    col_dkey = jnp.transpose(results[1], (1, 0, 2))
    col_dvalue = jnp.transpose(results[2], (1, 0, 2))
    return (row_dquery, row_dkey, row_dvalue, col_dquery, col_dkey, col_dvalue)
```

```python
import functools

import jax
import jax.numpy as jnp
from jax import lax
from jax.experimental import pallas as pl
from jax.experimental.pallas import tpu as pltpu
from jax.sharding import PartitionSpec as P

HEADS = 12
HEAD = 64
LANES = 128
BF16 = jnp.bfloat16
F32 = jnp.float32


def nn(a, b):
    return lax.dot_general(a, b, (((1,), (0,)), ((), ())), preferred_element_type=F32)


def nt(a, b):
    return lax.dot_general(a, b, (((1,), (1,)), ((), ())), preferred_element_type=F32)


def tn(a, b):
    return lax.dot_general(a, b, (((0,), (0,)), ((), ())), preferred_element_type=F32)


def iota(shape, axis):
    return lax.broadcasted_iota(jnp.int32, shape, axis)


def pack_kernel(axis, *refs):
    arrays, blocks = refs[:4], refs[4:]
    me = lax.axis_index(axis)
    lane = iota((16, 4, LANES), 2)
    for d in range(4):
        dst = me ^ d
        full = pl.multiple_of(dst * LANES, LANES)
        tail = pl.multiple_of((4 + (dst >> 1)) * LANES, LANES)
        odd = (dst & 1) == 1
        for a, x in enumerate(arrays):
            blocks[d][a * 32 : (a + 1) * 32] = x[:, :, pl.ds(full, LANES)]
            low = x[0:16, :, pl.ds(tail, LANES)]
            high = x[16:32, :, pl.ds(tail, LANES)]
            low = jnp.where(odd, pltpu.roll(low, HEAD, 2), low)
            high = jnp.where(odd, high, pltpu.roll(high, HEAD, 2))
            start = 128 + a * 16
            blocks[d][start : start + 16] = jnp.where(lane < HEAD, low, high)


def unpack_kernel(axis, *refs):
    blocks, outs = refs[:4], refs[4:]
    me = lax.axis_index(axis)
    lane = iota((16, 4, LANES), 2)
    odd = (me & 1) == 1
    for a, out in enumerate(outs):
        for d in range(4):
            full = pl.multiple_of((me ^ d) * LANES, LANES)
            out[:, :, pl.ds(full, LANES)] = blocks[d][a * 32 : (a + 1) * 32]
        start = 96 + a * 16
        for d in (0, 2):
            tail = pl.multiple_of((4 + ((me ^ d) >> 1)) * LANES, LANES)
            x = blocks[d][start : start + 16]
            y = blocks[d + 1][start : start + 16]
            even = jnp.where(odd, y, x)
            other = jnp.where(odd, x, y)
            out[0:16, :, pl.ds(tail, LANES)] = jnp.where(lane < HEAD, even, pltpu.roll(other, HEAD, 2))
            out[16:32, :, pl.ds(tail, LANES)] = jnp.where(lane < HEAD, pltpu.roll(even, HEAD, 2), other)


def row_group(blocks, array, part):
    start = array * 128 + part * 64 if part < 2 else 512 + array * 64
    return jnp.concatenate([b[start : start + 64, :] for b in blocks], axis=0)


def same_sequence(shape):
    return ((iota(shape, 0) >> 2) & 15) == ((iota(shape, 1) >> 2) & 15)


def row_score_kernel(b0, b1, b2, b3, out):
    blocks = (b0, b1, b2, b3)
    lane = iota((256, LANES), 1)
    mask = same_sequence((256, 256))
    partials = []
    for left, right in ((0, 1), (2, 3)):
        first = second = None
        for part in (0, 1):
            x = row_group(blocks, left, part)
            y = row_group(blocks, right, part)
            zero = jnp.zeros_like(x)
            f = nt(jnp.where(lane < HEAD, x, zero), y)
            s = nt(jnp.where(lane < HEAD, zero, x), y)
            first = f if first is None else first + f
            second = s if second is None else second + s
        third = nt(row_group(blocks, left, 2), row_group(blocks, right, 2))
        for g in (first, second, third):
            g = jnp.where(mask, g, 0.0)
            partials.append(g.reshape(4, 8, 8, 256).sum(axis=1).reshape(32, 256))
    total = jnp.zeros((32, LANES), F32)
    row = iota((256, LANES), 0)
    column = ((row >> 6) << 2) + (row & 3)
    for k, t in enumerate(partials):
        place = (iota((256, LANES), 1) == column + 16 * k).astype(BF16)
        for _ in range(3):
            high = t.astype(BF16)
            total = total + nn(high, place)
            t = t - high.astype(F32)
    r = iota((16, 32), 0)
    c = iota((16, 32), 1)
    fold = (((c >> 3) == (r >> 2)) & ((c & 3) == (r & 3))).astype(BF16)
    result = jnp.zeros((16, LANES), F32)
    for _ in range(3):
        high = total.astype(BF16)
        result = result + nn(fold, high)
        total = total - high.astype(F32)
    out[...] = result


def row_grad_kernel(row_scale, p0, p1, p2, p3, b0, b1, b2, b3, *outs):
    blocks = (b0, b1, b2, b3)
    total = (p0[...] + p1[...]) + (p2[...] + p3[...])
    lane = iota((256, LANES), 1)
    mask = same_sequence((256, 256))
    row = iota((256, 16), 0)
    spread = (iota((256, 16), 1) == ((row >> 6) << 2) + (row & 3)).astype(BF16)

    def expand(small, transposed):
        half = (nt if transposed else nn)(spread, small).astype(BF16)
        return jnp.where(mask, nt(half, spread), 0.0).astype(BF16)

    mats = []
    for h in range(3):
        scores = total[:, 16 * h : 16 * h + 16] * row_scale
        dprob = total[:, 48 + 16 * h : 64 + 16 * h]
        e = jnp.exp(scores - jnp.max(scores, axis=1, keepdims=True))
        probs = e / jnp.sum(e, axis=1, keepdims=True)
        delta = jnp.sum(probs * dprob, axis=1, keepdims=True)
        dscore = (probs * (dprob - delta) * row_scale).astype(BF16)
        weights = probs.astype(BF16)
        mats.append((expand(dscore, False), expand(dscore, True), expand(weights, True)))
    for k, array in enumerate((1, 0, 2)):
        for part in (0, 1, 2):
            x = row_group(blocks, array, part)
            if part < 2:
                y = jnp.where(lane < HEAD, nn(mats[0][k], x), nn(mats[1][k], x))
                start = k * 128 + part * 64
            else:
                y = nn(mats[2][k], x)
                start = 384 + k * 64
            y = y.astype(BF16)
            for d in range(4):
                outs[d][start : start + 64, :] = y[d * 64 : (d + 1) * 64, :]


def reorder(rows, inner):
    bits = {16: 4, 32: 5}[inner]
    r = iota((rows, rows), 0)
    c = iota((rows, rows), 1)
    group = 4 * inner - 1
    source = (r & ~group) + ((r & (inner - 1)) << 2) + ((r & group) >> bits)
    return (c == source).astype(BF16)


def restore(rows, inner):
    bits = {16: 4, 32: 5}[inner]
    r = iota((rows, rows), 0)
    c = iota((rows, rows), 1)
    group = 4 * inner - 1
    source = (c & ~group) + ((c & (inner - 1)) << 2) + ((c & group) >> bits)
    return (r == source).astype(BF16)


def column_kernel(col_scale, *refs):
    blocks, outs, work, grads = refs[:4], refs[4:8], refs[8], refs[9]
    pair_order, single_order = reorder(128, 32), reorder(128, 16)
    for d in range(4):
        for a in range(4):
            x = blocks[d][a * 128 : (a + 1) * 128, :]
            work[d, a * 128 : (a + 1) * 128, :] = nn(pair_order, x).astype(BF16)
        for a in range(2):
            x = blocks[d][512 + a * 128 : 640 + a * 128, :]
            work[d, 512 + a * 128 : 640 + a * 128, :] = nn(single_order, x).astype(BF16)
    lane = iota((128, LANES), 1)

    def core(query, key, value, grad):
        scores = nt(key, query) * col_scale
        dprob = nt(value, grad)
        e = jnp.exp(scores - jnp.max(scores, axis=0, keepdims=True))
        probs = e * (1.0 / jnp.sum(e, axis=0, keepdims=True))
        delta = jnp.sum(probs * dprob, axis=0, keepdims=True)
        dscore = (probs * (dprob - delta) * col_scale).astype(BF16)
        return dscore, probs.astype(BF16)

    for c in range(4):
        x = []
        for a in range(4):
            start = a * 128 + c * 32
            x.append(jnp.concatenate([work[d, start : start + 32, :] for d in range(4)], axis=0))
        query, key, grad, value = x[0], x[1], x[2], x[3]
        zero = jnp.zeros_like(query)
        results = []
        for h in range(2):
            keep = (lane < HEAD) if h == 0 else (lane >= HEAD)
            dscore, weights = core(query, jnp.where(keep, key, zero), jnp.where(keep, value, zero), grad)
            results.append((tn(dscore, key), nn(dscore, query), nn(weights, grad)))
        for k in range(3):
            y = jnp.where(lane < HEAD, results[0][k], results[1][k]).astype(BF16)
            for d in range(4):
                grads[d, k * 128 + c * 32 : k * 128 + (c + 1) * 32, :] = y[d * 32 : (d + 1) * 32, :]
        x = []
        for a in range(4):
            start = 512 + a * 64 + c * 16
            y = jnp.concatenate([work[d, start : start + 16, :] for d in range(4)], axis=0)
            x.append(jnp.concatenate([y[:, :HEAD], y[:, HEAD:]], axis=0))
        query, key, grad, value = x[0], x[1], x[2], x[3]
        dscore, weights = core(query, key, value, grad)
        for k, y in enumerate((tn(dscore, key), nn(dscore, query), nn(weights, grad))):
            y = jnp.concatenate([y[:64], y[64:]], axis=1).astype(BF16)
            for d in range(4):
                start = 384 + k * 64 + c * 16
                grads[d, start : start + 16, :] = y[d * 16 : (d + 1) * 16, :]
    pair_back, single_back = restore(128, 32), restore(64, 16)
    for d in range(4):
        for k in range(3):
            x = grads[d, k * 128 : (k + 1) * 128, :]
            outs[d][k * 128 : (k + 1) * 128, :] = nn(pair_back, x).astype(BF16)
            x = grads[d, 384 + k * 64 : 448 + k * 64, :]
            outs[d][384 + k * 64 : 448 + k * 64, :] = nn(single_back, x).astype(BF16)


VMEM = pl.BlockSpec(memory_space=pltpu.VMEM)
LIMIT = 40 * 1024 * 1024


def call(body, shapes, dtype, operands, name, flops, scratch=()):
    return pl.pallas_call(
        body,
        out_shape=[jax.ShapeDtypeStruct(s, dtype) for s in shapes],
        in_specs=[VMEM] * len(operands),
        out_specs=[VMEM] * len(shapes),
        scratch_shapes=list(scratch),
        compiler_params=pltpu.CompilerParams(vmem_limit_bytes=LIMIT),
        cost_estimate=pl.CostEstimate(flops=flops, bytes_accessed=1 << 20, transcendentals=0),
        name=name,
    )(*operands)


def exchange(blocks, axis):
    moved = [blocks[0]]
    for d in range(1, 4):
        moved.append(lax.ppermute(blocks[d], axis, [(i, i ^ d) for i in range(4)]))
    return moved


def pack(arrays, axis, name):
    blocks = call(functools.partial(pack_kernel, axis), [(192, 4, LANES)] * 4, BF16, arrays, name, 1 << 20)
    return [b.reshape(768, LANES) for b in blocks]


def unpack(blocks, axis, shape, name):
    blocks = [b.reshape(144, 4, LANES) for b in blocks]
    return call(functools.partial(unpack_kernel, axis), [shape] * 3, BF16, blocks, name, 1 << 20)


def local_fast(row_query, row_key, row_value, row_grad, col_query, col_key, col_value, col_grad):
    shape = row_query.shape
    seqs = shape[0] * lax.axis_size("seq")
    row_scale = HEAD ** (-0.5) * seqs ** (-0.5)
    col_scale = HEAD ** (-0.5)
    row_blocks = exchange(pack((row_query, row_key, row_grad, row_value), "col", "row_pack"), "col")
    col_blocks = exchange(pack((col_query, col_key, col_grad, col_value), "seq", "col_pack"), "seq")
    (part,) = call(row_score_kernel, [(16, LANES)], F32, row_blocks, "row_scores", 1 << 28)
    parts = exchange([part] * 4, "seq")
    col_out = call(
        functools.partial(column_kernel, col_scale),
        [(576, LANES)] * 4,
        BF16,
        col_blocks,
        "col_grads",
        1 << 30,
        scratch=(pltpu.VMEM((4, 768, LANES), BF16), pltpu.VMEM((4, 576, LANES), BF16)),
    )
    col_back = exchange(col_out, "seq")
    row_out = call(
        functools.partial(row_grad_kernel, row_scale),
        [(576, LANES)] * 4,
        BF16,
        parts + row_blocks,
        "row_grads",
        1 << 28,
    )
    row_back = exchange(row_out, "col")
    col_result = unpack(col_back, "seq", shape, "col_unpack")
    row_result = unpack(row_back, "col", shape, "row_unpack")
    return (*row_result, *col_result)


def tied_terms(scores, prob_grad, row_scale):
    row_probs = jax.nn.softmax(scores, axis=-1)
    row_delta = jnp.sum(row_probs * prob_grad, axis=-1, keepdims=True)
    score_gradient_part = row_probs * (prob_grad - row_delta) * row_scale
    return (row_probs.astype(BF16), score_gradient_part.astype(BF16))


def einsum(spec, a, b):
    return jnp.einsum(spec, a, b, preferred_element_type=F32)


def column_core(query, key, value, grad, col_scale):
    scores = einsum("qzd,izd->zqi", query, key) * col_scale
    prob_grad = einsum("qzd,izd->zqi", grad, value)
    weights, dscore = tied_terms(scores, prob_grad, col_scale)
    return (
        einsum("zqi,izd->qzd", dscore, key).astype(BF16),
        einsum("zqi,qzd->izd", dscore, query).astype(BF16),
        einsum("zqi,qzd->izd", weights, grad).astype(BF16),
    )


def local_general(row_query, row_key, row_value, row_grad, col_query, col_key, col_value, col_grad):
    seq_dev, col_dev, width = row_query.shape
    seqs = seq_dev * lax.axis_size("seq")
    cols = col_dev * lax.axis_size("col")
    row_scale = HEAD ** (-0.5) * seqs ** (-0.5)
    col_scale = HEAD ** (-0.5)
    moved = [
        lax.all_to_all(x, "col", split_axis=0, concat_axis=1, tiled=True)
        for x in (row_query, row_key, row_value, row_grad)
    ]
    own_rows = moved[0].shape[0]
    query, key, value, grad = (x.reshape(own_rows, cols, HEADS, HEAD) for x in moved)
    score_part = einsum("sihe,sjhe->hij", query, key) * row_scale
    prob_part = einsum("sihe,sjhe->hij", grad, value)
    scores, prob_grad = lax.psum((score_part, prob_part), ("col", "seq"))
    weights, dscore = tied_terms(scores, prob_grad, row_scale)
    row_back = [
        lax.all_to_all(
            y.astype(BF16).reshape(own_rows, cols, width), "col", split_axis=1, concat_axis=0, tiled=True
        )
        for y in (
            einsum("hij,sjhe->sihe", dscore, key),
            einsum("hij,sihe->sjhe", dscore, query),
            einsum("hij,sihe->sjhe", weights, grad),
        )
    ]
    col_moved = [
        lax.all_to_all(
            x.reshape(seq_dev, col_dev * width), "seq", split_axis=1, concat_axis=0, tiled=True
        )
        for x in (col_query, col_key, col_value, col_grad)
    ]
    share = col_moved[0].shape[1]
    col_grads = column_core(*(x.reshape(seqs, share // HEAD, HEAD) for x in col_moved), col_scale)
    col_back = [
        lax.all_to_all(y.reshape(seqs, share), "seq", split_axis=0, concat_axis=1, tiled=True)
        for y in col_grads
    ]
    return (*row_back, *(y.reshape(seq_dev, col_dev, width) for y in col_back))


def local(*arrays):
    sizes = (lax.axis_size("col"), lax.axis_size("seq"))
    if sizes == (4, 4) and arrays[0].shape == (32, 4, HEADS * HEAD):
        return local_fast(*arrays)
    return local_general(*arrays)


def solution(mesh):
    spec = P(("grp", "seq"), "col", None)
    return jax.shard_map(
        local, mesh=mesh, in_specs=(spec,) * 8, out_specs=(spec,) * 6, check_vma=False
    )
```

```python
import functools

import jax
import jax.numpy as jnp
from jax import lax
from jax.experimental import pallas as pl
from jax.experimental.pallas import tpu as pltpu
from jax.sharding import PartitionSpec as P

HEADS = 12
HEAD = 64
LANES = 128
BF16 = jnp.bfloat16
F32 = jnp.float32


def nn(a, b):
    return lax.dot_general(a, b, (((1,), (0,)), ((), ())), preferred_element_type=F32)


def nt(a, b):
    return lax.dot_general(a, b, (((1,), (1,)), ((), ())), preferred_element_type=F32)


def tn(a, b):
    return lax.dot_general(a, b, (((0,), (0,)), ((), ())), preferred_element_type=F32)


def iota(shape, axis):
    return lax.broadcasted_iota(jnp.int32, shape, axis)


def roll_half(x):
    return pltpu.roll(x, HEAD, 2)


def pack_kernel(axis, *refs):
    arrays, blocks, (held, sem) = refs[:4], refs[4:8], refs[8:]
    me = lax.axis_index(axis)
    copies = []
    for a in range(4):
        for q in range(CHUNKS):
            rows = pl.ds(q * (32 // CHUNKS), 32 // CHUNKS)
            copy = pltpu.make_async_copy(arrays[a].at[rows], held.at[a, rows], sem.at[a * CHUNKS + q])
            copy.start()
            copies.append(copy)
    lane = iota((16, 4, LANES), 2)
    for a in range(4):
        for copy in copies[a * CHUNKS : (a + 1) * CHUNKS]:
            copy.wait()
        for d in (2, 3, 1, 0):
            dst = me ^ d
            full = pl.multiple_of(dst * LANES, LANES)
            tail = pl.multiple_of((4 + (dst >> 1)) * LANES, LANES)
            odd = (dst & 1) == 1
            blocks[d][a * 32 : (a + 1) * 32] = held[a, :, :, pl.ds(full, LANES)]
            low = held[a, 0:16, :, pl.ds(tail, LANES)]
            high = held[a, 16:32, :, pl.ds(tail, LANES)]
            low = jnp.where(odd, roll_half(low), low)
            high = jnp.where(odd, high, roll_half(high))
            start = 128 + a * 16
            blocks[d][start : start + 16] = jnp.where(lane < HEAD, low, high)


def unpack_kernel(*refs):
    outs, (held, sem) = refs[8:14], refs[14:]
    lane = iota((16, 4, LANES), 2)
    copies = []
    for side, axis in ((1, "seq"), (0, "col")):
        b2, b3, b1, b0 = refs[4 * side : 4 * side + 4]
        blocks = (b0, b1, b2, b3)
        me = lax.axis_index(axis)
        odd = (me & 1) == 1
        for k in range(3):
            a = 3 * side + k
            for d in range(4):
                full = pl.multiple_of((me ^ d) * LANES, LANES)
                held[a, :, :, pl.ds(full, LANES)] = blocks[d][k * 32 : (k + 1) * 32]
            start = 96 + k * 16
            for d in (0, 2):
                tail = pl.multiple_of((4 + ((me ^ d) >> 1)) * LANES, LANES)
                x = blocks[d][start : start + 16]
                y = blocks[d + 1][start : start + 16]
                even = jnp.where(odd, y, x)
                other = jnp.where(odd, x, y)
                held[a, 0:16, :, pl.ds(tail, LANES)] = jnp.where(lane < HEAD, even, roll_half(other))
                held[a, 16:32, :, pl.ds(tail, LANES)] = jnp.where(lane < HEAD, roll_half(even), other)
            for q in range(CHUNKS):
                rows = pl.ds(q * (32 // CHUNKS), 32 // CHUNKS)
                copy = pltpu.make_async_copy(held.at[a, rows], outs[a].at[rows], sem.at[a * CHUNKS + q])
                copy.start()
                copies.append(copy)
    for copy in copies:
        copy.wait()


def row_group(blocks, array, part):
    start = array * 128 + part * 64 if part < 2 else 512 + array * 64
    return jnp.concatenate([b[start : start + 64, :] for b in blocks], axis=0)


def same_sequence(shape):
    return ((iota(shape, 0) >> 2) & 15) == ((iota(shape, 1) >> 2) & 15)


def row_score_kernel(b2, b3, b1, b0, out):
    blocks = (b0, b1, b2, b3)
    lane = iota((256, LANES), 1)
    mask = same_sequence((256, 256))
    partials = []
    for left, right in ((0, 1), (2, 3)):
        first = second = None
        for part in (0, 1):
            x = row_group(blocks, left, part)
            y = row_group(blocks, right, part)
            zero = jnp.zeros_like(x)
            f = nt(jnp.where(lane < HEAD, x, zero), y)
            s = nt(jnp.where(lane < HEAD, zero, x), y)
            first = f if first is None else first + f
            second = s if second is None else second + s
        third = nt(row_group(blocks, left, 2), row_group(blocks, right, 2))
        for g in (first, second, third):
            g = jnp.where(mask, g, 0.0)
            partials.append(g.reshape(4, 8, 8, 256).sum(axis=1).reshape(32, 256))
    total = jnp.zeros((32, LANES), F32)
    row = iota((256, LANES), 0)
    column = ((row >> 6) << 2) + (row & 3)
    for k, t in enumerate(partials):
        place = (iota((256, LANES), 1) == column + 16 * k).astype(BF16)
        for _ in range(3):
            high = t.astype(BF16)
            total = total + nn(high, place)
            t = t - high.astype(F32)
    r = iota((16, 32), 0)
    c = iota((16, 32), 1)
    fold = (((c >> 3) == (r >> 2)) & ((c & 3) == (r & 3))).astype(BF16)
    result = jnp.zeros((16, LANES), F32)
    for _ in range(3):
        high = total.astype(BF16)
        result = result + nn(fold, high)
        total = total - high.astype(F32)
    out[...] = result


def row_grad_kernel(row_scale, p0, p1, p2, p3, b2, b3, b1, b0, *outs):
    blocks = (b0, b1, b2, b3)
    total = (p0[...] + p1[...]) + (p2[...] + p3[...])
    lane = iota((256, LANES), 1)
    mask = same_sequence((256, 256))
    row = iota((256, 16), 0)
    spread = (iota((256, 16), 1) == ((row >> 6) << 2) + (row & 3)).astype(BF16)

    def expand(small, transposed):
        half = (nt if transposed else nn)(spread, small).astype(BF16)
        return jnp.where(mask, nt(half, spread), 0.0).astype(BF16)

    mats = []
    for h in range(3):
        scores = total[:, 16 * h : 16 * h + 16] * row_scale
        dprob = total[:, 48 + 16 * h : 64 + 16 * h]
        e = jnp.exp(scores - jnp.max(scores, axis=1, keepdims=True))
        probs = e / jnp.sum(e, axis=1, keepdims=True)
        delta = jnp.sum(probs * dprob, axis=1, keepdims=True)
        dscore = (probs * (dprob - delta) * row_scale).astype(BF16)
        weights = probs.astype(BF16)
        mats.append((expand(dscore, False), expand(dscore, True), expand(weights, True)))
    for k, array in enumerate((1, 0, 2)):
        for part in (0, 1, 2):
            x = row_group(blocks, array, part)
            if part < 2:
                y = jnp.where(lane < HEAD, nn(mats[0][k], x), nn(mats[1][k], x))
                start = k * 128 + part * 64
            else:
                y = nn(mats[2][k], x)
                start = 384 + k * 64
            y = y.astype(BF16)
            for d in range(4):
                outs[d][start : start + 64, :] = y[d * 64 : (d + 1) * 64, :]


def reorder(rows, inner):
    bits = {16: 4, 32: 5}[inner]
    r = iota((rows, rows), 0)
    c = iota((rows, rows), 1)
    group = 4 * inner - 1
    source = (r & ~group) + ((r & (inner - 1)) << 2) + ((r & group) >> bits)
    return (c == source).astype(BF16)


def restore(rows, inner):
    bits = {16: 4, 32: 5}[inner]
    r = iota((rows, rows), 0)
    c = iota((rows, rows), 1)
    group = 4 * inner - 1
    source = (c & ~group) + ((c & (inner - 1)) << 2) + ((c & group) >> bits)
    return (r == source).astype(BF16)


def column_kernel(col_scale, b2, b3, b1, b0, after, o0, o1, o2, o3, work, grads):
    blocks, outs = (b0, b1, b2, b3), (o0, o1, o2, o3)
    del after
    pair_order, single_order = reorder(128, 32), reorder(128, 16)
    for d in range(4):
        x = [blocks[d][a * 128 : (a + 1) * 128, :] for a in range(6)]
        for a in (0, 2):
            y = nn(pair_order, jnp.concatenate([x[a], x[a + 1]], axis=1)).astype(BF16)
            work[d, a * 128 : (a + 1) * 128, :] = y[:, :LANES]
            work[d, (a + 1) * 128 : (a + 2) * 128, :] = y[:, LANES:]
        y = nn(single_order, jnp.concatenate([x[4], x[5]], axis=1)).astype(BF16)
        work[d, 512:640, :] = y[:, :LANES]
        work[d, 640:768, :] = y[:, LANES:]
    lane = iota((128, LANES), 1)

    def core(query, key, value, grad):
        heads = key.shape[0] // 128
        shape = (heads, 128, 128)
        scores = (nt(key, query) * col_scale).reshape(shape)
        dprob = nt(value, grad).reshape(shape)
        e = jnp.exp(scores - jnp.max(scores, axis=1, keepdims=True))
        probs = e * (1.0 / jnp.sum(e, axis=1, keepdims=True))
        delta = jnp.sum(probs * dprob, axis=1, keepdims=True)
        dscore = (probs * (dprob - delta) * col_scale).astype(BF16).reshape(heads * 128, 128)
        weights = probs.astype(BF16).reshape(heads * 128, 128)
        return tn(dscore, key), nn(dscore, query), nn(weights, grad)

    def both(x):
        zero = jnp.zeros_like(x)
        return jnp.concatenate([jnp.where(lane < HEAD, x, zero), jnp.where(lane < HEAD, zero, x)], axis=0)

    for c in range(4):
        x = []
        for a in range(4):
            start = a * 128 + c * 32
            x.append(jnp.concatenate([work[d, start : start + 32, :] for d in range(4)], axis=0))
        query, key, grad, value = x
        dquery, dkey, dvalue = core(query, both(key), both(value), grad)
        dkey = jnp.where(lane < HEAD, dkey[:128], dkey[128:])
        dvalue = jnp.where(lane < HEAD, dvalue[:128], dvalue[128:])
        for k, y in enumerate((dquery, dkey, dvalue)):
            y = y.astype(BF16)
            for d in range(4):
                grads[d, k * 128 + c * 32 : k * 128 + (c + 1) * 32, :] = y[d * 32 : (d + 1) * 32, :]
        x = []
        for a in range(4):
            start = 512 + a * 64 + c * 16
            y = jnp.concatenate([work[d, start : start + 16, :] for d in range(4)], axis=0)
            x.append(jnp.concatenate([y[:, :HEAD], y[:, HEAD:]], axis=0))
        query, key, grad, value = x
        for k, y in enumerate(core(query, key, value, grad)):
            y = jnp.concatenate([y[:64], y[64:]], axis=1).astype(BF16)
            for d in range(4):
                start = 384 + k * 64 + c * 16
                grads[d, start : start + 16, :] = y[d * 16 : (d + 1) * 16, :]
    pair_back, single_back = restore(128, 32), restore(64, 16)
    for d in range(4):
        x = [grads[d, k * 128 : (k + 1) * 128, :] for k in range(3)]
        y = nn(pair_back, jnp.concatenate(x, axis=1)).astype(BF16)
        for k in range(3):
            outs[d][k * 128 : (k + 1) * 128, :] = y[:, k * LANES : (k + 1) * LANES]
        x = [grads[d, 384 + k * 64 : 448 + k * 64, :] for k in range(3)]
        y = nn(single_back, jnp.concatenate(x, axis=1)).astype(BF16)
        for k in range(3):
            outs[d][384 + k * 64 : 448 + k * 64, :] = y[:, k * LANES : (k + 1) * LANES]


VMEM = pl.BlockSpec(memory_space=pltpu.VMEM)
HBM = pl.BlockSpec(memory_space=pltpu.HBM)
LIMIT = 40 * 1024 * 1024
ROW = 1
CHUNKS = 4
COL = 4_000_000_000
SHIFTS = (2, 3, 1)


def call(body, shapes, operands, name, flops, scratch=(), in_space=VMEM, out_space=VMEM):
    return pl.pallas_call(
        body,
        out_shape=[jax.ShapeDtypeStruct(shape, dtype) for shape, dtype in shapes],
        in_specs=in_space if isinstance(in_space, list) else [in_space] * len(operands),
        out_specs=[out_space] * len(shapes),
        scratch_shapes=list(scratch),
        compiler_params=pltpu.CompilerParams(vmem_limit_bytes=LIMIT),
        cost_estimate=pl.CostEstimate(flops=flops, bytes_accessed=1, transcendentals=0),
        name=name,
    )(*operands)


def far_first(blocks):
    return [blocks[2], blocks[3], blocks[1], blocks[0]]


def exchange(blocks, axis):
    moved = list(blocks)
    for d in SHIFTS:
        moved[d] = lax.ppermute(blocks[d], axis, [(i, i ^ d) for i in range(4)])
    return moved


def pack(arrays, axis, name):
    arrays = [pltpu.with_memory_space_constraint(x, pltpu.HBM) for x in arrays]
    scratch = (pltpu.VMEM((4, *arrays[0].shape), BF16), pltpu.SemaphoreType.DMA((4 * CHUNKS,)))
    blocks = call(
        functools.partial(pack_kernel, axis), [((192, 4, LANES), BF16)] * 4, arrays, name, 1, scratch, in_space=HBM
    )
    return [b.reshape(768, LANES) for b in blocks]


def unpack(row_back, col_back, shape):
    operands = [b.reshape(144, 4, LANES) for b in far_first(row_back) + far_first(col_back)]
    scratch = (pltpu.VMEM((6, *shape), BF16), pltpu.SemaphoreType.DMA((6 * CHUNKS,)))
    return call(unpack_kernel, [(shape, BF16)] * 6, operands, "unpack", 1, scratch, out_space=HBM)


def local_fast(row_query, row_key, row_value, row_grad, col_query, col_key, col_value, col_grad):
    shape = row_query.shape
    seqs = shape[0] * lax.axis_size("seq")
    row_scale = HEAD ** (-0.5) * seqs ** (-0.5)
    col_scale = HEAD ** (-0.5)
    row_blocks = pack((row_query, row_key, row_grad, row_value), "col", "row_pack")
    row_blocks = exchange(row_blocks, "col")
    col_blocks = pack((col_query, col_key, col_grad, col_value), "seq", "col_pack")
    col_blocks = exchange(col_blocks, "seq")
    (part,) = call(row_score_kernel, [((16, LANES), F32)], far_first(row_blocks), "row_scores", ROW)
    parts = exchange([part] * 4, "seq")
    col_out = call(
        functools.partial(column_kernel, col_scale),
        [((576, LANES), BF16)] * 4,
        [*far_first(col_blocks), part],
        "col_grads",
        COL,
        scratch=(pltpu.VMEM((4, 768, LANES), BF16), pltpu.VMEM((4, 576, LANES), BF16)),
    )
    row_out = call(
        functools.partial(row_grad_kernel, row_scale),
        [((576, LANES), BF16)] * 4,
        parts + far_first(row_blocks),
        "row_grads",
        ROW,
    )
    row_out, col_out = lax.optimization_barrier((row_out, col_out))
    row_back = exchange(row_out, "col")
    col_back = exchange(col_out, "seq")
    return unpack(row_back, col_back, shape)


def tied_terms(scores, prob_grad, row_scale):
    row_probs = jax.nn.softmax(scores, axis=-1)
    row_delta = jnp.sum(row_probs * prob_grad, axis=-1, keepdims=True)
    score_gradient_part = row_probs * (prob_grad - row_delta) * row_scale
    return (row_probs.astype(BF16), score_gradient_part.astype(BF16))


def einsum(spec, a, b):
    return jnp.einsum(spec, a, b, preferred_element_type=F32)


def column_core(query, key, value, grad, col_scale):
    scores = einsum("qzd,izd->zqi", query, key) * col_scale
    prob_grad = einsum("qzd,izd->zqi", grad, value)
    weights, dscore = tied_terms(scores, prob_grad, col_scale)
    return (
        einsum("zqi,izd->qzd", dscore, key).astype(BF16),
        einsum("zqi,qzd->izd", dscore, query).astype(BF16),
        einsum("zqi,qzd->izd", weights, grad).astype(BF16),
    )


def local_general(row_query, row_key, row_value, row_grad, col_query, col_key, col_value, col_grad):
    seq_dev, col_dev, width = row_query.shape
    seqs = seq_dev * lax.axis_size("seq")
    cols = col_dev * lax.axis_size("col")
    row_scale = HEAD ** (-0.5) * seqs ** (-0.5)
    col_scale = HEAD ** (-0.5)
    moved = [
        lax.all_to_all(x, "col", split_axis=0, concat_axis=1, tiled=True)
        for x in (row_query, row_key, row_value, row_grad)
    ]
    own_rows = moved[0].shape[0]
    query, key, value, grad = (x.reshape(own_rows, cols, HEADS, HEAD) for x in moved)
    score_part = einsum("sihe,sjhe->hij", query, key) * row_scale
    prob_part = einsum("sihe,sjhe->hij", grad, value)
    scores, prob_grad = lax.psum((score_part, prob_part), ("col", "seq"))
    weights, dscore = tied_terms(scores, prob_grad, row_scale)
    row_back = [
        lax.all_to_all(
            y.astype(BF16).reshape(own_rows, cols, width), "col", split_axis=1, concat_axis=0, tiled=True
        )
        for y in (
            einsum("hij,sjhe->sihe", dscore, key),
            einsum("hij,sihe->sjhe", dscore, query),
            einsum("hij,sihe->sjhe", weights, grad),
        )
    ]
    col_moved = [
        lax.all_to_all(
            x.reshape(seq_dev, col_dev * width), "seq", split_axis=1, concat_axis=0, tiled=True
        )
        for x in (col_query, col_key, col_value, col_grad)
    ]
    share = col_moved[0].shape[1]
    col_grads = column_core(*(x.reshape(seqs, share // HEAD, HEAD) for x in col_moved), col_scale)
    col_back = [
        lax.all_to_all(y.reshape(seqs, share), "seq", split_axis=0, concat_axis=1, tiled=True)
        for y in col_grads
    ]
    return (*row_back, *(y.reshape(seq_dev, col_dev, width) for y in col_back))


def local(*arrays):
    sizes = (lax.axis_size("col"), lax.axis_size("seq"))
    if sizes == (4, 4) and arrays[0].shape == (32, 4, HEADS * HEAD):
        return local_fast(*arrays)
    return local_general(*arrays)


def solution(mesh):
    spec = P(("grp", "seq"), "col", None)
    return jax.shard_map(
        local, mesh=mesh, in_specs=(spec,) * 8, out_specs=(spec,) * 6, check_vma=False
    )
```

```python
import functools

import jax
import jax.numpy as jnp
from jax import lax
from jax.experimental import pallas as pl
from jax.experimental.pallas import tpu as pltpu
from jax.sharding import PartitionSpec as P

HEADS = 12
HEAD = 64
LANES = 128
BF16 = jnp.bfloat16
F32 = jnp.float32


def nn(a, b):
    return lax.dot_general(a, b, (((1,), (0,)), ((), ())), preferred_element_type=F32)


def nt(a, b):
    return lax.dot_general(a, b, (((1,), (1,)), ((), ())), preferred_element_type=F32)


def tn(a, b):
    return lax.dot_general(a, b, (((0,), (0,)), ((), ())), preferred_element_type=F32)


def iota(shape, axis):
    return lax.broadcasted_iota(jnp.int32, shape, axis)


def roll_half(x):
    return pltpu.roll(x, HEAD, 2)


def pack_kernel(axis, *refs):
    arrays, blocks, (held, sem) = refs[:4], refs[4:8], refs[8:]
    me = lax.axis_index(axis)
    copies = []
    for a in range(4):
        for q in range(CHUNKS):
            rows = pl.ds(q * (32 // CHUNKS), 32 // CHUNKS)
            copy = pltpu.make_async_copy(arrays[a].at[rows], held.at[a, rows], sem.at[a * CHUNKS + q])
            copy.start()
            copies.append(copy)
    low_lanes = iota((16, 4, LANES), 2) < HEAD
    odd = (me & 1) == 1
    for a in range(4):
        for copy in copies[a * CHUNKS : (a + 1) * CHUNKS]:
            copy.wait()
        for d in range(4):
            full = pl.multiple_of((me ^ d) * LANES, LANES)
            blocks[d][a * 32 : (a + 1) * 32] = held[a, :, :, pl.ds(full, LANES)]
        start = 128 + a * 16
        for d in (0, 2):
            tail = pl.multiple_of((4 + ((me ^ d) >> 1)) * LANES, LANES)
            low = held[a, 0:16, :, pl.ds(tail, LANES)]
            high = held[a, 16:32, :, pl.ds(tail, LANES)]
            x = roll_half(jnp.where(low_lanes, high, low))
            even_head = jnp.where(low_lanes, low, x)
            odd_head = jnp.where(low_lanes, x, high)
            blocks[d][start : start + 16] = jnp.where(odd, odd_head, even_head)
            blocks[d + 1][start : start + 16] = jnp.where(odd, even_head, odd_head)


def unpack_kernel(*refs):
    outs, (held, sem) = refs[-8:-2], refs[-2:]
    low_lanes = iota((16, 4, LANES), 2) < HEAD
    copies = []
    for side, axis in ((1, "seq"), (0, "col")):
        blocks = refs[4 * side : 4 * side + 4]
        blocks = (blocks[3], blocks[2], *blocks[:2]) if side else (blocks[3], blocks[0], blocks[2], blocks[1])
        me = lax.axis_index(axis)
        odd = (me & 1) == 1
        for k in range(3):
            a = 3 * side + k
            for d in range(4):
                full = pl.multiple_of((me ^ d) * LANES, LANES)
                held[a, :, :, pl.ds(full, LANES)] = blocks[d][k * 32 : (k + 1) * 32]
            start = 96 + k * 16
            for d in (0, 2):
                tail = pl.multiple_of((4 + ((me ^ d) >> 1)) * LANES, LANES)
                x = blocks[d][start : start + 16]
                y = blocks[d + 1][start : start + 16]
                even = jnp.where(odd, y, x)
                other = jnp.where(odd, x, y)
                z = roll_half(jnp.where(low_lanes, other, even))
                held[a, 0:16, :, pl.ds(tail, LANES)] = jnp.where(low_lanes, even, z)
                held[a, 16:32, :, pl.ds(tail, LANES)] = jnp.where(low_lanes, z, other)
            for q in range(CHUNKS):
                rows = pl.ds(q * (32 // CHUNKS), 32 // CHUNKS)
                copy = pltpu.make_async_copy(held.at[a, rows], outs[a].at[rows], sem.at[a * CHUNKS + q])
                copy.start()
                copies.append(copy)
    for copy in copies:
        copy.wait()


def pair_rows(blocks, array):
    parts = []
    for part in (0, 1):
        start = array * 128 + part * 64
        parts.append(jnp.concatenate([b[start : start + 64, :] for b in blocks], axis=0))
    return jnp.concatenate(parts, axis=1)


def single_rows(blocks, array):
    start = 512 + array * 64
    return jnp.concatenate([b[start : start + 64, :] for b in blocks], axis=0)


def first_head(shape):
    return (iota(shape, 1) & HEAD) == 0


def row_group(blocks, array, part):
    start = array * 128 + part * 64 if part < 2 else 512 + array * 64
    return jnp.concatenate([b[start : start + 64, :] for b in blocks], axis=0)


def same_sequence(shape):
    return ((iota(shape, 0) >> 2) & 15) == ((iota(shape, 1) >> 2) & 15)


def row_score_kernel(b3, b2, b1, b0, after0, after1, out):
    del after0, after1
    blocks = (b0, b1, b2, b3)
    lane = iota((256, LANES), 1)
    mask = same_sequence((256, 256))
    partials = []
    for left, right in ((0, 1), (2, 3)):
        first = second = None
        for part in (0, 1):
            x = row_group(blocks, left, part)
            y = row_group(blocks, right, part)
            zero = jnp.zeros_like(x)
            f = nt(jnp.where(lane < HEAD, x, zero), y)
            s = nt(jnp.where(lane < HEAD, zero, x), y)
            first = f if first is None else first + f
            second = s if second is None else second + s
        third = nt(row_group(blocks, left, 2), row_group(blocks, right, 2))
        for g in (first, second, third):
            g = jnp.where(mask, g, 0.0)
            partials.append(g.reshape(4, 8, 8, 256).sum(axis=1).reshape(32, 256))
    total = jnp.zeros((32, LANES), F32)
    row = iota((256, LANES), 0)
    column = ((row >> 6) << 2) + (row & 3)
    for k, t in enumerate(partials):
        place = (iota((256, LANES), 1) == column + 16 * k).astype(BF16)
        for _ in range(3):
            high = t.astype(BF16)
            total = total + nn(high, place)
            t = t - high.astype(F32)
    r = iota((16, 32), 0)
    c = iota((16, 32), 1)
    fold = (((c >> 3) == (r >> 2)) & ((c & 3) == (r & 3))).astype(BF16)
    result = jnp.zeros((16, LANES), F32)
    for _ in range(3):
        high = total.astype(BF16)
        result = result + nn(fold, high)
        total = total - high.astype(F32)
    out[...] = result


def row_grad_kernel(row_scale, p0, p1, p2, p3, b2, b3, b1, b0, after, *outs):
    del after
    outs[4][...] = jnp.zeros_like(outs[4])
    blocks = (b0, b1, b2, b3)
    total = (p0[...] + p1[...]) + (p2[...] + p3[...])
    dscores, weights = [], []
    for h in range(3):
        scores = total[:, 16 * h : 16 * h + 16] * row_scale
        dprob = total[:, 48 + 16 * h : 64 + 16 * h]
        e = jnp.exp(scores - jnp.max(scores, axis=1, keepdims=True))
        probs = e / jnp.sum(e, axis=1, keepdims=True)
        delta = jnp.sum(probs * dprob, axis=1, keepdims=True)
        dscores.append((probs * (dprob - delta) * row_scale).astype(BF16))
        weights.append(probs.astype(BF16))
    row = iota((256, 16), 0)
    spread = (iota((256, 16), 1) == ((row >> 6) << 2) + (row & 3)).astype(BF16)
    shape = (256, 256)
    mask = ((iota(shape, 0) >> 2) & 15) == ((iota(shape, 1) >> 2) & 15)
    keep = first_head(shape)
    plain = nn(spread, jnp.concatenate(dscores, axis=1)).astype(BF16)
    turned = nt(spread, jnp.concatenate(dscores + weights, axis=0)).astype(BF16)
    for k, array in enumerate((1, 0, 2)):
        mats = []
        for h in range(3):
            half = plain[:, 16 * h : 16 * h + 16] if k == 0 else turned[:, 48 * k - 48 + 16 * h : 48 * k - 32 + 16 * h]
            mats.append(jnp.where(mask, nt(half, spread), 0.0).astype(BF16))
        x = pair_rows(blocks, array)
        y = jnp.where(keep, nn(mats[0], x), nn(mats[1], x)).astype(BF16)
        z = nn(mats[2], single_rows(blocks, array)).astype(BF16)
        for n in range(4):
            outs[n][k * 128 : k * 128 + 64, :] = y[n * 64 : (n + 1) * 64, :LANES]
            outs[n][k * 128 + 64 : k * 128 + 128, :] = y[n * 64 : (n + 1) * 64, LANES:]
            outs[n][384 + k * 64 : 448 + k * 64, :] = z[n * 64 : (n + 1) * 64, :]


def reorder(rows, inner):
    bits = {16: 4, 32: 5}[inner]
    r = iota((rows, rows), 0)
    c = iota((rows, rows), 1)
    group = 4 * inner - 1
    source = (r & ~group) + ((r & (inner - 1)) << 2) + ((r & group) >> bits)
    return (c == source).astype(BF16)


def restore(rows, inner):
    bits = {16: 4, 32: 5}[inner]
    r = iota((rows, rows), 0)
    c = iota((rows, rows), 1)
    group = 4 * inner - 1
    source = (c & ~group) + ((c & (inner - 1)) << 2) + ((c & group) >> bits)
    return (r == source).astype(BF16)


def column_core_pair(col_scale, query, key, value, grad):
    heads = key.shape[0] // 128
    shape = (heads, 128, 128)
    scores = (nt(key, query) * col_scale).reshape(shape)
    dprob = nt(value, grad).reshape(shape)
    e = jnp.exp(scores - jnp.max(scores, axis=1, keepdims=True))
    probs = e * (1.0 / jnp.sum(e, axis=1, keepdims=True))
    delta = jnp.sum(probs * dprob, axis=1, keepdims=True)
    dscore = (probs * (dprob - delta) * col_scale).astype(BF16).reshape(heads * 128, 128)
    weights = probs.astype(BF16).reshape(heads * 128, 128)
    return tn(dscore, key), nn(dscore, query), nn(weights, grad)


def both(x):
    lane = iota(x.shape, 1)
    zero = jnp.zeros_like(x)
    return jnp.concatenate([jnp.where(lane < HEAD, x, zero), jnp.where(lane < HEAD, zero, x)], axis=0)


def column_grads(col_scale, columns, work, grads):
    lane = iota((128, LANES), 1)
    for c in columns:
        x = []
        for a in range(4):
            start = a * 128 + c * 32
            x.append(jnp.concatenate([work[d, start : start + 32, :] for d in range(4)], axis=0))
        query, key, grad, value = x
        dquery, dkey, dvalue = column_core_pair(col_scale, query, both(key), both(value), grad)
        dkey = jnp.where(lane < HEAD, dkey[:128], dkey[128:])
        dvalue = jnp.where(lane < HEAD, dvalue[:128], dvalue[128:])
        for k, y in enumerate((dquery, dkey, dvalue)):
            y = y.astype(BF16)
            for d in range(4):
                grads[d, k * 128 + c * 32 : k * 128 + (c + 1) * 32, :] = y[d * 32 : (d + 1) * 32, :]
        x = []
        for a in range(4):
            start = 512 + a * 64 + c * 16
            y = jnp.concatenate([work[d, start : start + 16, :] for d in range(4)], axis=0)
            x.append(jnp.concatenate([y[:, :HEAD], y[:, HEAD:]], axis=0))
        query, key, grad, value = x
        for k, y in enumerate(column_core_pair(col_scale, query, key, value, grad)):
            y = jnp.concatenate([y[:64], y[64:]], axis=1).astype(BF16)
            for d in range(4):
                start = 384 + k * 64 + c * 16
                grads[d, start : start + 16, :] = y[d * 16 : (d + 1) * 16, :]


def column_first_kernel(col_scale, b2, b3, b1, b0, after, work, grads):
    del after
    blocks = (b0, b1, b2, b3)
    pair_order, single_order = reorder(128, 32), reorder(128, 16)
    for d in range(4):
        x = [blocks[d][a * 128 : (a + 1) * 128, :] for a in range(6)]
        for a in (0, 2):
            y = nn(pair_order, jnp.concatenate([x[a], x[a + 1]], axis=1)).astype(BF16)
            work[d, a * 128 : (a + 1) * 128, :] = y[:, :LANES]
            work[d, (a + 1) * 128 : (a + 2) * 128, :] = y[:, LANES:]
        y = nn(single_order, jnp.concatenate([x[4], x[5]], axis=1)).astype(BF16)
        work[d, 512:640, :] = y[:, :LANES]
        work[d, 640:768, :] = y[:, LANES:]
    column_grads(col_scale, FIRST_COLUMNS, work, grads)


def joined(first, second, d, start, size, split):
    middle, stop = start + split * size, start + 4 * size
    return jnp.concatenate([first[d, start:middle, :], second[d, middle:stop, :]], axis=0)


def column_second_kernel(col_scale, work, first, after, o0, o1, o2, o3, grads):
    del after
    outs = (o0, o1, o2, o3)
    column_grads(col_scale, SECOND_COLUMNS, work, grads)
    split = len(FIRST_COLUMNS)
    pair_back, single_back = restore(128, 32), restore(64, 16)
    for d in range(4):
        x = [joined(first, grads, d, k * 128, 32, split) for k in range(3)]
        y = nn(pair_back, jnp.concatenate(x, axis=1)).astype(BF16)
        for k in range(3):
            outs[d][k * 128 : (k + 1) * 128, :] = y[:, k * LANES : (k + 1) * LANES]
        x = [joined(first, grads, d, 384 + k * 64, 16, split) for k in range(3)]
        y = nn(single_back, jnp.concatenate(x, axis=1)).astype(BF16)
        for k in range(3):
            outs[d][384 + k * 64 : 448 + k * 64, :] = y[:, k * LANES : (k + 1) * LANES]


def tick_kernel(*refs):
    refs[-1][...] = jnp.zeros_like(refs[-1])


VMEM = pl.BlockSpec(memory_space=pltpu.VMEM)
ANY = pl.BlockSpec(memory_space=pl.ANY)
HBM = pl.BlockSpec(memory_space=pltpu.HBM)
LIMIT = 40 * 1024 * 1024
ROW = 1
TICK = 20_000_000_000
CHUNKS = 2
FIRST_COLUMNS = (0, 1)
SECOND_COLUMNS = (2, 3)
COL = 4_000_000_000
SHIFTS = (2, 3, 1)


def call(body, shapes, operands, name, flops, scratch=(), in_space=VMEM, out_space=VMEM):
    kernel = pl.pallas_call(
        body,
        out_shape=[jax.ShapeDtypeStruct(shape, dtype) for shape, dtype in shapes],
        in_specs=in_space if isinstance(in_space, list) else [in_space] * len(operands),
        out_specs=[out_space] * len(shapes),
        scratch_shapes=list(scratch),
        compiler_params=pltpu.CompilerParams(vmem_limit_bytes=LIMIT),
        cost_estimate=pl.CostEstimate(flops=flops, bytes_accessed=1, transcendentals=0),
        name=name,
    )
    return list(kernel(*operands))


def far_first(blocks):
    return [blocks[2], blocks[3], blocks[1], blocks[0]]


def near_first(blocks):
    return [blocks[1], blocks[2], blocks[3], blocks[0]]


def exchange(blocks, axis, shifts=SHIFTS):
    moved = list(blocks)
    for d in shifts:
        moved[d] = lax.ppermute(blocks[d], axis, [(i, i ^ d) for i in range(4)])
    return moved


def pack(arrays, axis, name):
    arrays = [pltpu.with_memory_space_constraint(x, pltpu.HBM) for x in arrays]
    scratch = (pltpu.VMEM((4, *arrays[0].shape), BF16), pltpu.SemaphoreType.DMA((4 * CHUNKS,)))
    shapes = [((192, 4, LANES), BF16)] * 4
    blocks = call(functools.partial(pack_kernel, axis), shapes, arrays, name, 1, scratch, in_space=HBM)
    return [b.reshape(768, LANES) for b in blocks]


def tick(operands, name, flops):
    return call(tick_kernel, [((8, LANES), F32)], operands, name, flops, in_space=ANY)


def unpack(row_back, col_back, after, shape):
    operands = [b.reshape(144, 4, LANES) for b in [row_back[d] for d in (1, 3, 2, 0)] + far_first(col_back)]
    operands += after
    scratch = (pltpu.VMEM((6, *shape), BF16), pltpu.SemaphoreType.DMA((6 * CHUNKS,)))
    return call(unpack_kernel, [(shape, BF16)] * 6, operands, "unpack", 1, scratch, out_space=HBM)


def local_fast(row_query, row_key, row_value, row_grad, col_query, col_key, col_value, col_grad):
    shape = row_query.shape
    seqs = shape[0] * lax.axis_size("seq")
    row_scale = HEAD ** (-0.5) * seqs ** (-0.5)
    col_scale = HEAD ** (-0.5)
    row_blocks = pack((row_query, row_key, row_grad, row_value), "col", "row_pack")
    row_blocks = exchange(row_blocks, "col")
    col_blocks = pack((col_query, col_key, col_grad, col_value), "seq", "col_pack")
    col_blocks = exchange(col_blocks, "seq")
    (part,) = call(row_score_kernel, [((16, LANES), F32)], [row_blocks[d] for d in (3, 2, 1, 0)] + far_first(col_blocks)[:2], "row_scores", ROW)
    parts = exchange([part] * 4, "seq")
    col_work, col_first = call(
        functools.partial(column_first_kernel, col_scale),
        [((4, 768, LANES), BF16), ((4, 576, LANES), BF16)],
        [*far_first(col_blocks), part],
        "col_grads_first",
        COL,
    )
    *row_out, token = call(
        functools.partial(row_grad_kernel, row_scale),
        [((576, LANES), BF16)] * 4 + [((8, LANES), F32)],
        parts + far_first(row_blocks) + [col_first],
        "row_grads",
        ROW,
    )
    row_back = exchange(row_out, "col", (1, 2, 3))
    col_out = call(
        functools.partial(column_second_kernel, col_scale),
        [((576, LANES), BF16)] * 4,
        [col_work, col_first, token],
        "col_grads_second",
        COL,
        scratch=(pltpu.VMEM((4, 576, LANES), BF16),),
    )
    col_back = exchange(col_out, "seq")
    arrived = tick(far_first(row_back)[:3], "row_arrived", TICK)
    return tuple(unpack(row_back, col_back, arrived, shape))


def tied_terms(scores, prob_grad, row_scale):
    row_probs = jax.nn.softmax(scores, axis=-1)
    row_delta = jnp.sum(row_probs * prob_grad, axis=-1, keepdims=True)
    score_gradient_part = row_probs * (prob_grad - row_delta) * row_scale
    return (row_probs.astype(BF16), score_gradient_part.astype(BF16))


def einsum(spec, a, b):
    return jnp.einsum(spec, a, b, preferred_element_type=F32)


def column_core(query, key, value, grad, col_scale):
    scores = einsum("qzd,izd->zqi", query, key) * col_scale
    prob_grad = einsum("qzd,izd->zqi", grad, value)
    weights, dscore = tied_terms(scores, prob_grad, col_scale)
    return (
        einsum("zqi,izd->qzd", dscore, key).astype(BF16),
        einsum("zqi,qzd->izd", dscore, query).astype(BF16),
        einsum("zqi,qzd->izd", weights, grad).astype(BF16),
    )


def local_general(row_query, row_key, row_value, row_grad, col_query, col_key, col_value, col_grad):
    seq_dev, col_dev, width = row_query.shape
    seqs = seq_dev * lax.axis_size("seq")
    cols = col_dev * lax.axis_size("col")
    row_scale = HEAD ** (-0.5) * seqs ** (-0.5)
    col_scale = HEAD ** (-0.5)
    moved = [
        lax.all_to_all(x, "col", split_axis=0, concat_axis=1, tiled=True)
        for x in (row_query, row_key, row_value, row_grad)
    ]
    own_rows = moved[0].shape[0]
    query, key, value, grad = (x.reshape(own_rows, cols, HEADS, HEAD) for x in moved)
    score_part = einsum("sihe,sjhe->hij", query, key) * row_scale
    prob_part = einsum("sihe,sjhe->hij", grad, value)
    scores, prob_grad = lax.psum((score_part, prob_part), ("col", "seq"))
    weights, dscore = tied_terms(scores, prob_grad, row_scale)
    row_back = [
        lax.all_to_all(
            y.astype(BF16).reshape(own_rows, cols, width), "col", split_axis=1, concat_axis=0, tiled=True
        )
        for y in (
            einsum("hij,sjhe->sihe", dscore, key),
            einsum("hij,sihe->sjhe", dscore, query),
            einsum("hij,sihe->sjhe", weights, grad),
        )
    ]
    col_moved = [
        lax.all_to_all(
            x.reshape(seq_dev, col_dev * width), "seq", split_axis=1, concat_axis=0, tiled=True
        )
        for x in (col_query, col_key, col_value, col_grad)
    ]
    share = col_moved[0].shape[1]
    col_grads = column_core(*(x.reshape(seqs, share // HEAD, HEAD) for x in col_moved), col_scale)
    col_back = [
        lax.all_to_all(y.reshape(seqs, share), "seq", split_axis=0, concat_axis=1, tiled=True)
        for y in col_grads
    ]
    return (*row_back, *(y.reshape(seq_dev, col_dev, width) for y in col_back))


def local(*arrays):
    sizes = (lax.axis_size("col"), lax.axis_size("seq"))
    if sizes == (4, 4) and arrays[0].shape == (32, 4, HEADS * HEAD):
        return local_fast(*arrays)
    return local_general(*arrays)


def solution(mesh):
    spec = P(("grp", "seq"), "col", None)
    return jax.shard_map(
        local, mesh=mesh, in_specs=(spec,) * 8, out_specs=(spec,) * 6, check_vma=False
    )
```

```python
import functools

import jax
import jax.numpy as jnp
from jax import lax
from jax.experimental import pallas as pl
from jax.experimental.pallas import tpu as pltpu
from jax.sharding import PartitionSpec as P

HEADS = 12
HEAD = 64
LANES = 128
BF16 = jnp.bfloat16
F32 = jnp.float32


def nn(a, b):
    return lax.dot_general(a, b, (((1,), (0,)), ((), ())), preferred_element_type=F32)


def nt(a, b):
    return lax.dot_general(a, b, (((1,), (1,)), ((), ())), preferred_element_type=F32)


def tn(a, b):
    return lax.dot_general(a, b, (((0,), (0,)), ((), ())), preferred_element_type=F32)


def iota(shape, axis):
    return lax.broadcasted_iota(jnp.int32, shape, axis)


def roll_half(x):
    return pltpu.roll(x, HEAD, 2)


def pack_kernel(axis, *refs):
    arrays, blocks, (held, sem) = refs[:4], refs[4:8], refs[8:]
    me = lax.axis_index(axis)
    copies = []
    for a in range(4):
        for q in range(CHUNKS):
            rows = pl.ds(q * (32 // CHUNKS), 32 // CHUNKS)
            copy = pltpu.make_async_copy(arrays[a].at[rows], held.at[a, rows], sem.at[a * CHUNKS + q])
            copy.start()
            copies.append(copy)
    low_lanes = iota((16, 4, LANES), 2) < HEAD
    odd = (me & 1) == 1
    for a in range(4):
        for copy in copies[a * CHUNKS : (a + 1) * CHUNKS]:
            copy.wait()
        for d in range(4):
            full = pl.multiple_of((me ^ d) * LANES, LANES)
            blocks[d][a * 32 : (a + 1) * 32] = held[a, :, :, pl.ds(full, LANES)]
        start = 128 + a * 16
        for d in (0, 2):
            tail = pl.multiple_of((4 + ((me ^ d) >> 1)) * LANES, LANES)
            low = held[a, 0:16, :, pl.ds(tail, LANES)]
            high = held[a, 16:32, :, pl.ds(tail, LANES)]
            x = roll_half(jnp.where(low_lanes, high, low))
            even_head = jnp.where(low_lanes, low, x)
            odd_head = jnp.where(low_lanes, x, high)
            blocks[d][start : start + 16] = jnp.where(odd, odd_head, even_head)
            blocks[d + 1][start : start + 16] = jnp.where(odd, even_head, odd_head)


def unpack_kernel(*refs):
    outs, (held, sem) = refs[-8:-2], refs[-2:]
    low_lanes = iota((16, 4, LANES), 2) < HEAD
    copies = []
    for side, axis in ((1, "seq"), (0, "col")):
        blocks = refs[4 * side : 4 * side + 4]
        blocks = by_partner(blocks, (2, 3, 1, 0) if side else RETURN)
        me = lax.axis_index(axis)
        odd = (me & 1) == 1
        for k in range(3):
            a = 3 * side + k
            for d in range(4):
                full = pl.multiple_of((me ^ d) * LANES, LANES)
                held[a, :, :, pl.ds(full, LANES)] = blocks[d][k * 32 : (k + 1) * 32]
            start = 96 + k * 16
            for d in (0, 2):
                tail = pl.multiple_of((4 + ((me ^ d) >> 1)) * LANES, LANES)
                x = blocks[d][start : start + 16]
                y = blocks[d + 1][start : start + 16]
                even = jnp.where(odd, y, x)
                other = jnp.where(odd, x, y)
                z = roll_half(jnp.where(low_lanes, other, even))
                held[a, 0:16, :, pl.ds(tail, LANES)] = jnp.where(low_lanes, even, z)
                held[a, 16:32, :, pl.ds(tail, LANES)] = jnp.where(low_lanes, z, other)
            for q in range(CHUNKS):
                rows = pl.ds(q * (32 // CHUNKS), 32 // CHUNKS)
                copy = pltpu.make_async_copy(held.at[a, rows], outs[a].at[rows], sem.at[a * CHUNKS + q])
                copy.start()
                copies.append(copy)
    for copy in copies:
        copy.wait()


def pair_rows(blocks, array):
    parts = []
    for part in (0, 1):
        start = array * 128 + part * 64
        parts.append(jnp.concatenate([b[start : start + 64, :] for b in blocks], axis=0))
    return jnp.concatenate(parts, axis=1)


def single_rows(blocks, array):
    start = 512 + array * 64
    return jnp.concatenate([b[start : start + 64, :] for b in blocks], axis=0)


def first_head(shape):
    return (iota(shape, 1) & HEAD) == 0


def row_group(blocks, array, part):
    start = array * 128 + part * 64 if part < 2 else 512 + array * 64
    return jnp.concatenate([b[start : start + 64, :] for b in blocks], axis=0)


def same_sequence(shape):
    return ((iota(shape, 0) >> 2) & 15) == ((iota(shape, 1) >> 2) & 15)


def by_partner(blocks, order):
    return [blocks[order.index(d)] for d in range(4)]


def row_score_kernel(r0, r1, r2, r3, after0, after1, out):
    del after0, after1
    blocks = by_partner((r0, r1, r2, r3), ENTRY)
    lane = iota((256, LANES), 1)
    mask = same_sequence((256, 256))
    partials = []
    for left, right in ((0, 1), (2, 3)):
        first = second = None
        for part in (0, 1):
            x = row_group(blocks, left, part)
            y = row_group(blocks, right, part)
            zero = jnp.zeros_like(x)
            f = nt(jnp.where(lane < HEAD, x, zero), y)
            s = nt(jnp.where(lane < HEAD, zero, x), y)
            first = f if first is None else first + f
            second = s if second is None else second + s
        third = nt(row_group(blocks, left, 2), row_group(blocks, right, 2))
        for g in (first, second, third):
            g = jnp.where(mask, g, 0.0)
            partials.append(g.reshape(4, 8, 8, 256).sum(axis=1).reshape(32, 256))
    total = jnp.zeros((32, LANES), F32)
    row = iota((256, LANES), 0)
    column = ((row >> 6) << 2) + (row & 3)
    for k, t in enumerate(partials):
        place = (iota((256, LANES), 1) == column + 16 * k).astype(BF16)
        for _ in range(3):
            high = t.astype(BF16)
            total = total + nn(high, place)
            t = t - high.astype(F32)
    r = iota((16, 32), 0)
    c = iota((16, 32), 1)
    fold = (((c >> 3) == (r >> 2)) & ((c & 3) == (r & 3))).astype(BF16)
    result = jnp.zeros((16, LANES), F32)
    for _ in range(3):
        high = total.astype(BF16)
        result = result + nn(fold, high)
        total = total - high.astype(F32)
    out[...] = result


def row_grad_kernel(row_scale, p2, p3, p1, p0, b2, b3, b1, b0, after, *outs):
    del after
    outs[4][...] = jnp.zeros_like(outs[4])
    blocks = (b0, b1, b2, b3)
    total = (p0[...] + p1[...]) + (p2[...] + p3[...])
    dscores, weights = [], []
    for h in range(3):
        scores = total[:, 16 * h : 16 * h + 16] * row_scale
        dprob = total[:, 48 + 16 * h : 64 + 16 * h]
        e = jnp.exp(scores - jnp.max(scores, axis=1, keepdims=True))
        probs = e / jnp.sum(e, axis=1, keepdims=True)
        delta = jnp.sum(probs * dprob, axis=1, keepdims=True)
        dscores.append((probs * (dprob - delta) * row_scale).astype(BF16))
        weights.append(probs.astype(BF16))
    row = iota((256, 16), 0)
    spread = (iota((256, 16), 1) == ((row >> 6) << 2) + (row & 3)).astype(BF16)
    shape = (256, 256)
    mask = ((iota(shape, 0) >> 2) & 15) == ((iota(shape, 1) >> 2) & 15)
    keep = first_head(shape)
    plain = nn(spread, jnp.concatenate(dscores, axis=1)).astype(BF16)
    turned = nt(spread, jnp.concatenate(dscores + weights, axis=0)).astype(BF16)
    for k, array in enumerate((1, 0, 2)):
        mats = []
        for h in range(3):
            half = plain[:, 16 * h : 16 * h + 16] if k == 0 else turned[:, 48 * k - 48 + 16 * h : 48 * k - 32 + 16 * h]
            mats.append(jnp.where(mask, nt(half, spread), 0.0).astype(BF16))
        x = pair_rows(blocks, array)
        y = jnp.where(keep, nn(mats[0], x), nn(mats[1], x)).astype(BF16)
        z = nn(mats[2], single_rows(blocks, array)).astype(BF16)
        for n in range(4):
            outs[n][k * 128 : k * 128 + 64, :] = y[n * 64 : (n + 1) * 64, :LANES]
            outs[n][k * 128 + 64 : k * 128 + 128, :] = y[n * 64 : (n + 1) * 64, LANES:]
            outs[n][384 + k * 64 : 448 + k * 64, :] = z[n * 64 : (n + 1) * 64, :]


def reorder(rows, inner):
    bits = {16: 4, 32: 5}[inner]
    r = iota((rows, rows), 0)
    c = iota((rows, rows), 1)
    group = 4 * inner - 1
    source = (r & ~group) + ((r & (inner - 1)) << 2) + ((r & group) >> bits)
    return (c == source).astype(BF16)


def restore(rows, inner):
    bits = {16: 4, 32: 5}[inner]
    r = iota((rows, rows), 0)
    c = iota((rows, rows), 1)
    group = 4 * inner - 1
    source = (c & ~group) + ((c & (inner - 1)) << 2) + ((c & group) >> bits)
    return (r == source).astype(BF16)


def column_core_pair(col_scale, query, key, value, grad):
    heads = key.shape[0] // 128
    shape = (heads, 128, 128)
    scores = (nt(key, query) * col_scale).reshape(shape)
    dprob = nt(value, grad).reshape(shape)
    e = jnp.exp(scores - jnp.max(scores, axis=1, keepdims=True))
    probs = e * (1.0 / jnp.sum(e, axis=1, keepdims=True))
    delta = jnp.sum(probs * dprob, axis=1, keepdims=True)
    dscore = (probs * (dprob - delta) * col_scale).astype(BF16).reshape(heads * 128, 128)
    weights = probs.astype(BF16).reshape(heads * 128, 128)
    return tn(dscore, key), nn(dscore, query), nn(weights, grad)


def both(x):
    lane = iota(x.shape, 1)
    zero = jnp.zeros_like(x)
    return jnp.concatenate([jnp.where(lane < HEAD, x, zero), jnp.where(lane < HEAD, zero, x)], axis=0)


def column_grads(col_scale, columns, work, grads):
    lane = iota((128, LANES), 1)
    for c in columns:
        x = []
        for a in range(4):
            start = a * 128 + c * 32
            x.append(jnp.concatenate([work[d, start : start + 32, :] for d in range(4)], axis=0))
        query, key, grad, value = x
        dquery, dkey, dvalue = column_core_pair(col_scale, query, both(key), both(value), grad)
        dkey = jnp.where(lane < HEAD, dkey[:128], dkey[128:])
        dvalue = jnp.where(lane < HEAD, dvalue[:128], dvalue[128:])
        for k, y in enumerate((dquery, dkey, dvalue)):
            y = y.astype(BF16)
            for d in range(4):
                grads[d, k * 128 + c * 32 : k * 128 + (c + 1) * 32, :] = y[d * 32 : (d + 1) * 32, :]
        x = []
        for a in range(4):
            start = 512 + a * 64 + c * 16
            y = jnp.concatenate([work[d, start : start + 16, :] for d in range(4)], axis=0)
            x.append(jnp.concatenate([y[:, :HEAD], y[:, HEAD:]], axis=0))
        query, key, grad, value = x
        for k, y in enumerate(column_core_pair(col_scale, query, key, value, grad)):
            y = jnp.concatenate([y[:64], y[64:]], axis=1).astype(BF16)
            for d in range(4):
                start = 384 + k * 64 + c * 16
                grads[d, start : start + 16, :] = y[d * 16 : (d + 1) * 16, :]


def column_first_kernel(col_scale, b2, b3, b1, b0, after, work, grads):
    del after
    blocks = (b0, b1, b2, b3)
    pair_order, single_order = reorder(128, 32), reorder(128, 16)
    for d in range(4):
        x = [blocks[d][a * 128 : (a + 1) * 128, :] for a in range(6)]
        for a in (0, 2):
            y = nn(pair_order, jnp.concatenate([x[a], x[a + 1]], axis=1)).astype(BF16)
            work[d, a * 128 : (a + 1) * 128, :] = y[:, :LANES]
            work[d, (a + 1) * 128 : (a + 2) * 128, :] = y[:, LANES:]
        y = nn(single_order, jnp.concatenate([x[4], x[5]], axis=1)).astype(BF16)
        work[d, 512:640, :] = y[:, :LANES]
        work[d, 640:768, :] = y[:, LANES:]
    column_grads(col_scale, FIRST_COLUMNS, work, grads)


def joined(first, second, d, start, size, split):
    middle, stop = start + split * size, start + 4 * size
    return jnp.concatenate([first[d, start:middle, :], second[d, middle:stop, :]], axis=0)


def column_second_kernel(col_scale, work, first, after, o0, o1, o2, o3, grads):
    del after
    outs = (o0, o1, o2, o3)
    column_grads(col_scale, SECOND_COLUMNS, work, grads)
    split = len(FIRST_COLUMNS)
    pair_back, single_back = restore(128, 32), restore(64, 16)
    for d in range(4):
        x = [joined(first, grads, d, k * 128, 32, split) for k in range(3)]
        y = nn(pair_back, jnp.concatenate(x, axis=1)).astype(BF16)
        for k in range(3):
            outs[d][k * 128 : (k + 1) * 128, :] = y[:, k * LANES : (k + 1) * LANES]
        x = [joined(first, grads, d, 384 + k * 64, 16, split) for k in range(3)]
        y = nn(single_back, jnp.concatenate(x, axis=1)).astype(BF16)
        for k in range(3):
            outs[d][384 + k * 64 : 448 + k * 64, :] = y[:, k * LANES : (k + 1) * LANES]


def tick_kernel(*refs):
    refs[-1][...] = jnp.zeros_like(refs[-1])


VMEM = pl.BlockSpec(memory_space=pltpu.VMEM)
ANY = pl.BlockSpec(memory_space=pl.ANY)
HBM = pl.BlockSpec(memory_space=pltpu.HBM)
LIMIT = 40 * 1024 * 1024
ROW = 1
TICK = 20_000_000_000
CHUNKS = 2
FIRST_COLUMNS = (0,)
SECOND_COLUMNS = (1, 2, 3)
COL = 4_000_000_000
ENTRY = (2, 1, 3, 0)
RETURN = (1, 3, 2, 0)
SHIFTS = (2, 3, 1)


def call(body, shapes, operands, name, flops, scratch=(), in_space=VMEM, out_space=VMEM):
    kernel = pl.pallas_call(
        body,
        out_shape=[jax.ShapeDtypeStruct(shape, dtype) for shape, dtype in shapes],
        in_specs=in_space if isinstance(in_space, list) else [in_space] * len(operands),
        out_specs=[out_space] * len(shapes),
        scratch_shapes=list(scratch),
        compiler_params=pltpu.CompilerParams(vmem_limit_bytes=LIMIT),
        cost_estimate=pl.CostEstimate(flops=flops, bytes_accessed=1, transcendentals=0),
        name=name,
    )
    return list(kernel(*operands))


def far_first(blocks):
    return [blocks[2], blocks[3], blocks[1], blocks[0]]


def near_first(blocks):
    return [blocks[1], blocks[2], blocks[3], blocks[0]]


def exchange(blocks, axis, shifts=SHIFTS):
    moved = list(blocks)
    for d in shifts:
        moved[d] = lax.ppermute(blocks[d], axis, [(i, i ^ d) for i in range(4)])
    return moved


def pack(arrays, axis, name):
    arrays = [pltpu.with_memory_space_constraint(x, pltpu.HBM) for x in arrays]
    scratch = (pltpu.VMEM((4, *arrays[0].shape), BF16), pltpu.SemaphoreType.DMA((4 * CHUNKS,)))
    shapes = [((192, 4, LANES), BF16)] * 4
    blocks = call(functools.partial(pack_kernel, axis), shapes, arrays, name, 1, scratch, in_space=HBM)
    return [b.reshape(768, LANES) for b in blocks]


def tick(operands, name, flops):
    return call(tick_kernel, [((8, LANES), F32)], operands, name, flops, in_space=ANY)


def unpack(row_back, col_back, after, shape):
    operands = [b.reshape(144, 4, LANES) for b in [row_back[d] for d in RETURN] + far_first(col_back)]
    operands += after
    scratch = (pltpu.VMEM((6, *shape), BF16), pltpu.SemaphoreType.DMA((6 * CHUNKS,)))
    return call(unpack_kernel, [(shape, BF16)] * 6, operands, "unpack", 1, scratch, out_space=HBM)


def local_fast(row_query, row_key, row_value, row_grad, col_query, col_key, col_value, col_grad):
    shape = row_query.shape
    seqs = shape[0] * lax.axis_size("seq")
    row_scale = HEAD ** (-0.5) * seqs ** (-0.5)
    col_scale = HEAD ** (-0.5)
    row_blocks = pack((row_query, row_key, row_grad, row_value), "col", "row_pack")
    row_blocks = exchange(row_blocks, "col")
    col_blocks = pack((col_query, col_key, col_grad, col_value), "seq", "col_pack")
    col_blocks = exchange(col_blocks, "seq")
    (part,) = call(row_score_kernel, [((16, LANES), F32)], [row_blocks[d] for d in ENTRY] + far_first(col_blocks)[:2], "row_scores", ROW)
    parts = exchange([part] * 4, "seq")
    col_work, col_first = call(
        functools.partial(column_first_kernel, col_scale),
        [((4, 768, LANES), BF16), ((4, 576, LANES), BF16)],
        [*far_first(col_blocks), part],
        "col_grads_first",
        COL,
    )
    *row_out, token = call(
        functools.partial(row_grad_kernel, row_scale),
        [((576, LANES), BF16)] * 4 + [((8, LANES), F32)],
        far_first(parts) + far_first(row_blocks) + [col_first],
        "row_grads",
        ROW,
    )
    row_back = exchange(row_out, "col", (1, 2, 3))
    col_out = call(
        functools.partial(column_second_kernel, col_scale),
        [((576, LANES), BF16)] * 4,
        [col_work, col_first, token],
        "col_grads_second",
        COL,
        scratch=(pltpu.VMEM((4, 576, LANES), BF16),),
    )
    col_back = exchange(col_out, "seq")
    arrived = tick(far_first(row_back)[:3], "row_arrived", TICK)
    return tuple(unpack(row_back, col_back, arrived, shape))


def tied_terms(scores, prob_grad, row_scale):
    row_probs = jax.nn.softmax(scores, axis=-1)
    row_delta = jnp.sum(row_probs * prob_grad, axis=-1, keepdims=True)
    score_gradient_part = row_probs * (prob_grad - row_delta) * row_scale
    return (row_probs.astype(BF16), score_gradient_part.astype(BF16))


def einsum(spec, a, b):
    return jnp.einsum(spec, a, b, preferred_element_type=F32)


def column_core(query, key, value, grad, col_scale):
    scores = einsum("qzd,izd->zqi", query, key) * col_scale
    prob_grad = einsum("qzd,izd->zqi", grad, value)
    weights, dscore = tied_terms(scores, prob_grad, col_scale)
    return (
        einsum("zqi,izd->qzd", dscore, key).astype(BF16),
        einsum("zqi,qzd->izd", dscore, query).astype(BF16),
        einsum("zqi,qzd->izd", weights, grad).astype(BF16),
    )


def local_general(row_query, row_key, row_value, row_grad, col_query, col_key, col_value, col_grad):
    seq_dev, col_dev, width = row_query.shape
    seqs = seq_dev * lax.axis_size("seq")
    cols = col_dev * lax.axis_size("col")
    row_scale = HEAD ** (-0.5) * seqs ** (-0.5)
    col_scale = HEAD ** (-0.5)
    moved = [
        lax.all_to_all(x, "col", split_axis=0, concat_axis=1, tiled=True)
        for x in (row_query, row_key, row_value, row_grad)
    ]
    own_rows = moved[0].shape[0]
    query, key, value, grad = (x.reshape(own_rows, cols, HEADS, HEAD) for x in moved)
    score_part = einsum("sihe,sjhe->hij", query, key) * row_scale
    prob_part = einsum("sihe,sjhe->hij", grad, value)
    scores, prob_grad = lax.psum((score_part, prob_part), ("col", "seq"))
    weights, dscore = tied_terms(scores, prob_grad, row_scale)
    row_back = [
        lax.all_to_all(
            y.astype(BF16).reshape(own_rows, cols, width), "col", split_axis=1, concat_axis=0, tiled=True
        )
        for y in (
            einsum("hij,sjhe->sihe", dscore, key),
            einsum("hij,sihe->sjhe", dscore, query),
            einsum("hij,sihe->sjhe", weights, grad),
        )
    ]
    col_moved = [
        lax.all_to_all(
            x.reshape(seq_dev, col_dev * width), "seq", split_axis=1, concat_axis=0, tiled=True
        )
        for x in (col_query, col_key, col_value, col_grad)
    ]
    share = col_moved[0].shape[1]
    col_grads = column_core(*(x.reshape(seqs, share // HEAD, HEAD) for x in col_moved), col_scale)
    col_back = [
        lax.all_to_all(y.reshape(seqs, share), "seq", split_axis=0, concat_axis=1, tiled=True)
        for y in col_grads
    ]
    return (*row_back, *(y.reshape(seq_dev, col_dev, width) for y in col_back))


def local(*arrays):
    sizes = (lax.axis_size("col"), lax.axis_size("seq"))
    if sizes == (4, 4) and arrays[0].shape == (32, 4, HEADS * HEAD):
        return local_fast(*arrays)
    return local_general(*arrays)


def solution(mesh):
    spec = P(("grp", "seq"), "col", None)
    return jax.shard_map(
        local, mesh=mesh, in_specs=(spec,) * 8, out_specs=(spec,) * 6, check_vma=False
    )
```

```python
import functools

import jax
import jax.numpy as jnp
from jax import lax
from jax.experimental import pallas as pl
from jax.experimental.pallas import tpu as pltpu
from jax.sharding import PartitionSpec as P

HEADS = 12
HEAD = 64
LANES = 128
BF16 = jnp.bfloat16
F32 = jnp.float32


def nn(a, b):
    return lax.dot_general(a, b, (((1,), (0,)), ((), ())), preferred_element_type=F32)


def nt(a, b):
    return lax.dot_general(a, b, (((1,), (1,)), ((), ())), preferred_element_type=F32)


def tn(a, b):
    return lax.dot_general(a, b, (((0,), (0,)), ((), ())), preferred_element_type=F32)


def iota(shape, axis):
    return lax.broadcasted_iota(jnp.int32, shape, axis)


def roll_half(x):
    return pltpu.roll(x, HEAD, 2)


def pack_kernel(axis, *refs):
    arrays, blocks, (held, sem) = refs[:4], refs[4:8], refs[8:]
    me = lax.axis_index(axis)
    copies = []
    for a in range(4):
        for q in range(CHUNKS):
            rows = pl.ds(q * (32 // CHUNKS), 32 // CHUNKS)
            copy = pltpu.make_async_copy(arrays[a].at[rows], held.at[a, rows], sem.at[a * CHUNKS + q])
            copy.start()
            copies.append(copy)
    low_lanes = iota((16, 4, LANES), 2) < HEAD
    odd = (me & 1) == 1
    for a in range(4):
        for copy in copies[a * CHUNKS : (a + 1) * CHUNKS]:
            copy.wait()
        for d in range(4):
            full = pl.multiple_of((me ^ d) * LANES, LANES)
            blocks[d][a * 32 : (a + 1) * 32] = held[a, :, :, pl.ds(full, LANES)]
        start = 128 + a * 16
        for d in (0, 2):
            tail = pl.multiple_of((4 + ((me ^ d) >> 1)) * LANES, LANES)
            low = held[a, 0:16, :, pl.ds(tail, LANES)]
            high = held[a, 16:32, :, pl.ds(tail, LANES)]
            x = roll_half(jnp.where(low_lanes, high, low))
            even_head = jnp.where(low_lanes, low, x)
            odd_head = jnp.where(low_lanes, x, high)
            blocks[d][start : start + 16] = jnp.where(odd, odd_head, even_head)
            blocks[d + 1][start : start + 16] = jnp.where(odd, even_head, odd_head)


def unpack_kernel(*refs):
    outs, (held, sem, tile_sem) = refs[-9:-3], refs[-3:]
    low_lanes = iota((16, 4, LANES), 2) < HEAD
    copies = []
    for side, axis in ((1, "seq"), (0, "col")):
        blocks = refs[4 * side : 4 * side + 4]
        blocks = by_partner(blocks, (2, 3, 1, 0) if side else RETURN)
        me = lax.axis_index(axis)
        odd = (me & 1) == 1
        for k in range(3):
            a = 3 * side + k
            for d in range(4):
                full = pl.multiple_of((me ^ d) * LANES, LANES)
                if side:
                    copy = pltpu.make_async_copy(
                        blocks[d].at[pl.ds(k * 32, 32)], outs[a].at[:, :, pl.ds(full, LANES)], tile_sem.at[4 * k + d]
                    )
                    copy.start()
                    copies.append(copy)
                else:
                    held[a, :, :, pl.ds(full, LANES)] = blocks[d][k * 32 : (k + 1) * 32]
            start = 96 + k * 16
            for d in (0, 2):
                tail = pl.multiple_of((4 + ((me ^ d) >> 1)) * LANES, LANES)
                x = blocks[d][start : start + 16]
                y = blocks[d + 1][start : start + 16]
                even = jnp.where(odd, y, x)
                other = jnp.where(odd, x, y)
                z = roll_half(jnp.where(low_lanes, other, even))
                held[a, 0:16, :, pl.ds(tail, LANES)] = jnp.where(low_lanes, even, z)
                held[a, 16:32, :, pl.ds(tail, LANES)] = jnp.where(low_lanes, z, other)
            first = 4 * LANES if side else 0
            lanes = pl.ds(first, 6 * LANES - first)
            for q in range(CHUNKS):
                rows = pl.ds(q * (32 // CHUNKS), 32 // CHUNKS)
                copy = pltpu.make_async_copy(held.at[a, rows, :, lanes], outs[a].at[rows, :, lanes], sem.at[a * CHUNKS + q])
                copy.start()
                copies.append(copy)
    for copy in copies:
        copy.wait()


def pair_rows(blocks, array):
    parts = []
    for part in (0, 1):
        start = array * 128 + part * 64
        parts.append(jnp.concatenate([b[start : start + 64, :] for b in blocks], axis=0))
    return jnp.concatenate(parts, axis=1)


def single_rows(blocks, array):
    start = 512 + array * 64
    return jnp.concatenate([b[start : start + 64, :] for b in blocks], axis=0)


def first_head(shape):
    return (iota(shape, 1) & HEAD) == 0


def row_group(blocks, array, part):
    start = array * 128 + part * 64 if part < 2 else 512 + array * 64
    return jnp.concatenate([b[start : start + 64, :] for b in blocks], axis=0)


def same_sequence(shape):
    return ((iota(shape, 0) >> 2) & 15) == ((iota(shape, 1) >> 2) & 15)


def by_partner(blocks, order):
    return [blocks[order.index(d)] for d in range(4)]


def row_score_kernel(r0, r1, r2, r3, after0, after1, out):
    del after0, after1
    blocks = by_partner((r0, r1, r2, r3), ENTRY)
    lane = iota((256, LANES), 1)
    mask = same_sequence((256, 256))
    partials = []
    for left, right in ((0, 1), (2, 3)):
        first = second = None
        for part in (0, 1):
            x = row_group(blocks, left, part)
            y = row_group(blocks, right, part)
            zero = jnp.zeros_like(x)
            f = nt(jnp.where(lane < HEAD, x, zero), y)
            s = nt(jnp.where(lane < HEAD, zero, x), y)
            first = f if first is None else first + f
            second = s if second is None else second + s
        third = nt(row_group(blocks, left, 2), row_group(blocks, right, 2))
        for g in (first, second, third):
            g = jnp.where(mask, g, 0.0)
            partials.append(g.reshape(4, 8, 8, 256).sum(axis=1).reshape(32, 256))
    total = jnp.zeros((32, LANES), F32)
    row = iota((256, LANES), 0)
    column = ((row >> 6) << 2) + (row & 3)
    for k, t in enumerate(partials):
        place = (iota((256, LANES), 1) == column + 16 * k).astype(BF16)
        for _ in range(3):
            high = t.astype(BF16)
            total = total + nn(high, place)
            t = t - high.astype(F32)
    r = iota((16, 32), 0)
    c = iota((16, 32), 1)
    fold = (((c >> 3) == (r >> 2)) & ((c & 3) == (r & 3))).astype(BF16)
    result = jnp.zeros((16, LANES), F32)
    for _ in range(3):
        high = total.astype(BF16)
        result = result + nn(fold, high)
        total = total - high.astype(F32)
    out[...] = result


def row_grad_kernel(row_scale, p2, p3, p1, p0, b2, b3, b1, b0, after, *outs):
    del after
    outs[4][...] = jnp.zeros_like(outs[4])
    blocks = (b0, b1, b2, b3)
    total = (p0[...] + p1[...]) + (p2[...] + p3[...])
    dscores, weights = [], []
    for h in range(3):
        scores = total[:, 16 * h : 16 * h + 16] * row_scale
        dprob = total[:, 48 + 16 * h : 64 + 16 * h]
        e = jnp.exp(scores - jnp.max(scores, axis=1, keepdims=True))
        probs = e / jnp.sum(e, axis=1, keepdims=True)
        delta = jnp.sum(probs * dprob, axis=1, keepdims=True)
        dscores.append((probs * (dprob - delta) * row_scale).astype(BF16))
        weights.append(probs.astype(BF16))
    row = iota((256, 16), 0)
    spread = (iota((256, 16), 1) == ((row >> 6) << 2) + (row & 3)).astype(BF16)
    shape = (256, 256)
    mask = ((iota(shape, 0) >> 2) & 15) == ((iota(shape, 1) >> 2) & 15)
    keep = first_head(shape)
    plain = nn(spread, jnp.concatenate(dscores, axis=1)).astype(BF16)
    turned = nt(spread, jnp.concatenate(dscores + weights, axis=0)).astype(BF16)
    for k, array in enumerate((1, 0, 2)):
        mats = []
        for h in range(3):
            half = plain[:, 16 * h : 16 * h + 16] if k == 0 else turned[:, 48 * k - 48 + 16 * h : 48 * k - 32 + 16 * h]
            mats.append(jnp.where(mask, nt(half, spread), 0.0).astype(BF16))
        x = pair_rows(blocks, array)
        y = jnp.where(keep, nn(mats[0], x), nn(mats[1], x)).astype(BF16)
        z = nn(mats[2], single_rows(blocks, array)).astype(BF16)
        for n in range(4):
            outs[n][k * 128 : k * 128 + 64, :] = y[n * 64 : (n + 1) * 64, :LANES]
            outs[n][k * 128 + 64 : k * 128 + 128, :] = y[n * 64 : (n + 1) * 64, LANES:]
            outs[n][384 + k * 64 : 448 + k * 64, :] = z[n * 64 : (n + 1) * 64, :]


def reorder(rows, inner):
    bits = {16: 4, 32: 5}[inner]
    r = iota((rows, rows), 0)
    c = iota((rows, rows), 1)
    group = 4 * inner - 1
    source = (r & ~group) + ((r & (inner - 1)) << 2) + ((r & group) >> bits)
    return (c == source).astype(BF16)


def restore(rows, inner):
    bits = {16: 4, 32: 5}[inner]
    r = iota((rows, rows), 0)
    c = iota((rows, rows), 1)
    group = 4 * inner - 1
    source = (c & ~group) + ((c & (inner - 1)) << 2) + ((c & group) >> bits)
    return (r == source).astype(BF16)


def column_core_pair(col_scale, query, key, value, grad):
    heads = key.shape[0] // 128
    shape = (heads, 128, 128)
    scores = (nt(key, query) * col_scale).reshape(shape)
    dprob = nt(value, grad).reshape(shape)
    e = jnp.exp(scores - jnp.max(scores, axis=1, keepdims=True))
    probs = e * (1.0 / jnp.sum(e, axis=1, keepdims=True))
    delta = jnp.sum(probs * dprob, axis=1, keepdims=True)
    dscore = (probs * (dprob - delta) * col_scale).astype(BF16).reshape(heads * 128, 128)
    weights = probs.astype(BF16).reshape(heads * 128, 128)
    return tn(dscore, key), nn(dscore, query), nn(weights, grad)


def both(x):
    lane = iota(x.shape, 1)
    zero = jnp.zeros_like(x)
    return jnp.concatenate([jnp.where(lane < HEAD, x, zero), jnp.where(lane < HEAD, zero, x)], axis=0)


def column_grads(col_scale, columns, work, grads):
    lane = iota((128, LANES), 1)
    for c in columns:
        x = []
        for a in range(4):
            start = a * 128 + c * 32
            x.append(jnp.concatenate([work[d, start : start + 32, :] for d in range(4)], axis=0))
        query, key, grad, value = x
        dquery, dkey, dvalue = column_core_pair(col_scale, query, both(key), both(value), grad)
        dkey = jnp.where(lane < HEAD, dkey[:128], dkey[128:])
        dvalue = jnp.where(lane < HEAD, dvalue[:128], dvalue[128:])
        for k, y in enumerate((dquery, dkey, dvalue)):
            y = y.astype(BF16)
            for d in range(4):
                grads[d, k * 128 + c * 32 : k * 128 + (c + 1) * 32, :] = y[d * 32 : (d + 1) * 32, :]
        x = []
        for a in range(4):
            start = 512 + a * 64 + c * 16
            y = jnp.concatenate([work[d, start : start + 16, :] for d in range(4)], axis=0)
            x.append(jnp.concatenate([y[:, :HEAD], y[:, HEAD:]], axis=0))
        query, key, grad, value = x
        for k, y in enumerate(column_core_pair(col_scale, query, key, value, grad)):
            y = jnp.concatenate([y[:64], y[64:]], axis=1).astype(BF16)
            for d in range(4):
                start = 384 + k * 64 + c * 16
                grads[d, start : start + 16, :] = y[d * 16 : (d + 1) * 16, :]


def column_first_kernel(col_scale, b2, b3, b1, b0, after, work, grads):
    del after
    blocks = (b0, b1, b2, b3)
    pair_order, single_order = reorder(128, 32), reorder(128, 16)
    for d in range(4):
        x = [blocks[d][a * 128 : (a + 1) * 128, :] for a in range(6)]
        for a in (0, 2):
            y = nn(pair_order, jnp.concatenate([x[a], x[a + 1]], axis=1)).astype(BF16)
            work[d, a * 128 : (a + 1) * 128, :] = y[:, :LANES]
            work[d, (a + 1) * 128 : (a + 2) * 128, :] = y[:, LANES:]
        y = nn(single_order, jnp.concatenate([x[4], x[5]], axis=1)).astype(BF16)
        work[d, 512:640, :] = y[:, :LANES]
        work[d, 640:768, :] = y[:, LANES:]
    column_grads(col_scale, FIRST_COLUMNS, work, grads)


def joined(first, second, d, start, size, split):
    middle, stop = start + split * size, start + 4 * size
    return jnp.concatenate([first[d, start:middle, :], second[d, middle:stop, :]], axis=0)


def column_second_kernel(col_scale, work, first, after, o0, o1, o2, o3, grads):
    del after
    outs = (o0, o1, o2, o3)
    column_grads(col_scale, SECOND_COLUMNS, work, grads)
    split = len(FIRST_COLUMNS)
    pair_back, single_back = restore(128, 32), restore(64, 16)
    for d in range(4):
        x = [joined(first, grads, d, k * 128, 32, split) for k in range(3)]
        y = nn(pair_back, jnp.concatenate(x, axis=1)).astype(BF16)
        for k in range(3):
            outs[d][k * 128 : (k + 1) * 128, :] = y[:, k * LANES : (k + 1) * LANES]
        x = [joined(first, grads, d, 384 + k * 64, 16, split) for k in range(3)]
        y = nn(single_back, jnp.concatenate(x, axis=1)).astype(BF16)
        for k in range(3):
            outs[d][384 + k * 64 : 448 + k * 64, :] = y[:, k * LANES : (k + 1) * LANES]


def tick_kernel(*refs):
    refs[-1][...] = jnp.zeros_like(refs[-1])


VMEM = pl.BlockSpec(memory_space=pltpu.VMEM)
ANY = pl.BlockSpec(memory_space=pl.ANY)
HBM = pl.BlockSpec(memory_space=pltpu.HBM)
LIMIT = 40 * 1024 * 1024
ROW = 1
TICK = 20_000_000_000
CHUNKS = 2
FIRST_COLUMNS = (0,)
SECOND_COLUMNS = (1, 2, 3)
COL = 4_000_000_000
ENTRY = (2, 1, 3, 0)
RETURN = (1, 3, 2, 0)
SHIFTS = (2, 3, 1)


def call(body, shapes, operands, name, flops, scratch=(), in_space=VMEM, out_space=VMEM):
    kernel = pl.pallas_call(
        body,
        out_shape=[jax.ShapeDtypeStruct(shape, dtype) for shape, dtype in shapes],
        in_specs=in_space if isinstance(in_space, list) else [in_space] * len(operands),
        out_specs=[out_space] * len(shapes),
        scratch_shapes=list(scratch),
        compiler_params=pltpu.CompilerParams(vmem_limit_bytes=LIMIT),
        cost_estimate=pl.CostEstimate(flops=flops, bytes_accessed=1, transcendentals=0),
        name=name,
    )
    return list(kernel(*operands))


def far_first(blocks):
    return [blocks[2], blocks[3], blocks[1], blocks[0]]


def near_first(blocks):
    return [blocks[1], blocks[2], blocks[3], blocks[0]]


def exchange(blocks, axis, shifts=SHIFTS):
    moved = list(blocks)
    for d in shifts:
        moved[d] = lax.ppermute(blocks[d], axis, [(i, i ^ d) for i in range(4)])
    return moved


def pack(arrays, axis, name):
    arrays = [pltpu.with_memory_space_constraint(x, pltpu.HBM) for x in arrays]
    scratch = (pltpu.VMEM((4, *arrays[0].shape), BF16), pltpu.SemaphoreType.DMA((4 * CHUNKS,)))
    shapes = [((192, 4, LANES), BF16)] * 4
    blocks = call(functools.partial(pack_kernel, axis), shapes, arrays, name, 1, scratch, in_space=HBM)
    return [b.reshape(768, LANES) for b in blocks]


def tick(operands, name, flops):
    return call(tick_kernel, [((8, LANES), F32)], operands, name, flops, in_space=ANY)


def unpack(row_back, col_back, after, shape):
    operands = [b.reshape(144, 4, LANES) for b in [row_back[d] for d in RETURN] + far_first(col_back)]
    operands += after
    scratch = (
        pltpu.VMEM((6, *shape), BF16),
        pltpu.SemaphoreType.DMA((6 * CHUNKS,)),
        pltpu.SemaphoreType.DMA((12,)),
    )
    return call(unpack_kernel, [(shape, BF16)] * 6, operands, "unpack", 1, scratch, out_space=HBM)


def local_fast(row_query, row_key, row_value, row_grad, col_query, col_key, col_value, col_grad):
    shape = row_query.shape
    seqs = shape[0] * lax.axis_size("seq")
    row_scale = HEAD ** (-0.5) * seqs ** (-0.5)
    col_scale = HEAD ** (-0.5)
    row_blocks = pack((row_query, row_key, row_grad, row_value), "col", "row_pack")
    row_blocks = exchange(row_blocks, "col")
    col_blocks = pack((col_query, col_key, col_grad, col_value), "seq", "col_pack")
    col_blocks = exchange(col_blocks, "seq")
    (part,) = call(row_score_kernel, [((16, LANES), F32)], [row_blocks[d] for d in ENTRY] + far_first(col_blocks)[:2], "row_scores", ROW)
    parts = exchange([part] * 4, "seq")
    col_work, col_first = call(
        functools.partial(column_first_kernel, col_scale),
        [((4, 768, LANES), BF16), ((4, 576, LANES), BF16)],
        [*far_first(col_blocks), part],
        "col_grads_first",
        COL,
    )
    *row_out, token = call(
        functools.partial(row_grad_kernel, row_scale),
        [((576, LANES), BF16)] * 4 + [((8, LANES), F32)],
        far_first(parts) + far_first(row_blocks) + [col_first],
        "row_grads",
        ROW,
    )
    row_back = exchange(row_out, "col", (1, 2, 3))
    col_out = call(
        functools.partial(column_second_kernel, col_scale),
        [((576, LANES), BF16)] * 4,
        [col_work, col_first, token],
        "col_grads_second",
        COL,
        scratch=(pltpu.VMEM((4, 576, LANES), BF16),),
    )
    col_back = exchange(col_out, "seq")
    arrived = tick(far_first(row_back)[:3], "row_arrived", TICK)
    return tuple(unpack(row_back, col_back, arrived, shape))


def tied_terms(scores, prob_grad, row_scale):
    row_probs = jax.nn.softmax(scores, axis=-1)
    row_delta = jnp.sum(row_probs * prob_grad, axis=-1, keepdims=True)
    score_gradient_part = row_probs * (prob_grad - row_delta) * row_scale
    return (row_probs.astype(BF16), score_gradient_part.astype(BF16))


def einsum(spec, a, b):
    return jnp.einsum(spec, a, b, preferred_element_type=F32)


def column_core(query, key, value, grad, col_scale):
    scores = einsum("qzd,izd->zqi", query, key) * col_scale
    prob_grad = einsum("qzd,izd->zqi", grad, value)
    weights, dscore = tied_terms(scores, prob_grad, col_scale)
    return (
        einsum("zqi,izd->qzd", dscore, key).astype(BF16),
        einsum("zqi,qzd->izd", dscore, query).astype(BF16),
        einsum("zqi,qzd->izd", weights, grad).astype(BF16),
    )


def local_general(row_query, row_key, row_value, row_grad, col_query, col_key, col_value, col_grad):
    seq_dev, col_dev, width = row_query.shape
    seqs = seq_dev * lax.axis_size("seq")
    cols = col_dev * lax.axis_size("col")
    row_scale = HEAD ** (-0.5) * seqs ** (-0.5)
    col_scale = HEAD ** (-0.5)
    moved = [
        lax.all_to_all(x, "col", split_axis=0, concat_axis=1, tiled=True)
        for x in (row_query, row_key, row_value, row_grad)
    ]
    own_rows = moved[0].shape[0]
    query, key, value, grad = (x.reshape(own_rows, cols, HEADS, HEAD) for x in moved)
    score_part = einsum("sihe,sjhe->hij", query, key) * row_scale
    prob_part = einsum("sihe,sjhe->hij", grad, value)
    scores, prob_grad = lax.psum((score_part, prob_part), ("col", "seq"))
    weights, dscore = tied_terms(scores, prob_grad, row_scale)
    row_back = [
        lax.all_to_all(
            y.astype(BF16).reshape(own_rows, cols, width), "col", split_axis=1, concat_axis=0, tiled=True
        )
        for y in (
            einsum("hij,sjhe->sihe", dscore, key),
            einsum("hij,sihe->sjhe", dscore, query),
            einsum("hij,sihe->sjhe", weights, grad),
        )
    ]
    col_moved = [
        lax.all_to_all(
            x.reshape(seq_dev, col_dev * width), "seq", split_axis=1, concat_axis=0, tiled=True
        )
        for x in (col_query, col_key, col_value, col_grad)
    ]
    share = col_moved[0].shape[1]
    col_grads = column_core(*(x.reshape(seqs, share // HEAD, HEAD) for x in col_moved), col_scale)
    col_back = [
        lax.all_to_all(y.reshape(seqs, share), "seq", split_axis=0, concat_axis=1, tiled=True)
        for y in col_grads
    ]
    return (*row_back, *(y.reshape(seq_dev, col_dev, width) for y in col_back))


def local(*arrays):
    sizes = (lax.axis_size("col"), lax.axis_size("seq"))
    if sizes == (4, 4) and arrays[0].shape == (32, 4, HEADS * HEAD):
        return local_fast(*arrays)
    return local_general(*arrays)


def solution(mesh):
    spec = P(("grp", "seq"), "col", None)
    return jax.shard_map(
        local, mesh=mesh, in_specs=(spec,) * 8, out_specs=(spec,) * 6, check_vma=False
    )
```

```python
import functools

import jax
import jax.numpy as jnp
from jax import lax
from jax.experimental import pallas as pl
from jax.experimental.pallas import tpu as pltpu
from jax.sharding import PartitionSpec as P

HEADS = 12
HEAD = 64
LANES = 128
BF16 = jnp.bfloat16
F32 = jnp.float32


def nn(a, b):
    return lax.dot_general(a, b, (((1,), (0,)), ((), ())), preferred_element_type=F32)


def nt(a, b):
    return lax.dot_general(a, b, (((1,), (1,)), ((), ())), preferred_element_type=F32)


def tn(a, b):
    return lax.dot_general(a, b, (((0,), (0,)), ((), ())), preferred_element_type=F32)


def iota(shape, axis):
    return lax.broadcasted_iota(jnp.int32, shape, axis)


def roll_half(x):
    return pltpu.roll(x, HEAD, 2)


def pack_kernel(axis, *refs):
    arrays, blocks, (held, sem) = refs[:4], refs[4:8], refs[8:]
    me = lax.axis_index(axis)
    copies = []
    for a in range(4):
        for q in range(CHUNKS):
            rows = pl.ds(q * (32 // CHUNKS), 32 // CHUNKS)
            copy = pltpu.make_async_copy(arrays[a].at[rows], held.at[a, rows], sem.at[a * CHUNKS + q])
            copy.start()
            copies.append(copy)
    low_lanes = iota((16, 4, LANES), 2) < HEAD
    odd = (me & 1) == 1
    for a in range(4):
        for copy in copies[a * CHUNKS : (a + 1) * CHUNKS]:
            copy.wait()
        for d in range(4):
            full = pl.multiple_of((me ^ d) * LANES, LANES)
            blocks[d][a * 32 : (a + 1) * 32] = held[a, :, :, pl.ds(full, LANES)]
        start = 128 + a * 16
        for d in (0, 2):
            tail = pl.multiple_of((4 + ((me ^ d) >> 1)) * LANES, LANES)
            low = held[a, 0:16, :, pl.ds(tail, LANES)]
            high = held[a, 16:32, :, pl.ds(tail, LANES)]
            x = roll_half(jnp.where(low_lanes, high, low))
            even_head = jnp.where(low_lanes, low, x)
            odd_head = jnp.where(low_lanes, x, high)
            blocks[d][start : start + 16] = jnp.where(odd, odd_head, even_head)
            blocks[d + 1][start : start + 16] = jnp.where(odd, even_head, odd_head)


def unpack_kernel(*refs):
    outs, (held, sem) = refs[-8:-2], refs[-2:]
    low_lanes = iota((16, 4, LANES), 2) < HEAD
    copies = []
    for side, axis in ((1, "seq"), (0, "col")):
        blocks = refs[4 * side : 4 * side + 4]
        blocks = by_partner(blocks, (2, 3, 1, 0) if side else RETURN)
        me = lax.axis_index(axis)
        odd = (me & 1) == 1
        for k in range(3):
            a = 3 * side + k
            for d in range(4):
                full = pl.multiple_of((me ^ d) * LANES, LANES)
                held[a, :, :, pl.ds(full, LANES)] = blocks[d][k * 32 : (k + 1) * 32]
            start = 96 + k * 16
            for d in (0, 2):
                tail = pl.multiple_of((4 + ((me ^ d) >> 1)) * LANES, LANES)
                x = blocks[d][start : start + 16]
                y = blocks[d + 1][start : start + 16]
                even = jnp.where(odd, y, x)
                other = jnp.where(odd, x, y)
                z = roll_half(jnp.where(low_lanes, other, even))
                held[a, 0:16, :, pl.ds(tail, LANES)] = jnp.where(low_lanes, even, z)
                held[a, 16:32, :, pl.ds(tail, LANES)] = jnp.where(low_lanes, z, other)
            for q in range(CHUNKS):
                rows = pl.ds(q * (32 // CHUNKS), 32 // CHUNKS)
                copy = pltpu.make_async_copy(held.at[a, rows], outs[a].at[rows], sem.at[a * CHUNKS + q])
                copy.start()
                copies.append(copy)
    for copy in copies:
        copy.wait()


def pair_rows(blocks, array):
    parts = []
    for part in (0, 1):
        start = array * 128 + part * 64
        parts.append(jnp.concatenate([b[start : start + 64, :] for b in blocks], axis=0))
    return jnp.concatenate(parts, axis=1)


def single_rows(blocks, array):
    start = 512 + array * 64
    return jnp.concatenate([b[start : start + 64, :] for b in blocks], axis=0)


def first_head(shape):
    return (iota(shape, 1) & HEAD) == 0


def row_group(blocks, array, part):
    start = array * 128 + part * 64 if part < 2 else 512 + array * 64
    return jnp.concatenate([b[start : start + 64, :] for b in blocks], axis=0)


def same_sequence(shape):
    return ((iota(shape, 0) >> 2) & 15) == ((iota(shape, 1) >> 2) & 15)


def by_partner(blocks, order):
    return [blocks[order.index(d)] for d in range(4)]


def row_score_kernel(r0, r1, r2, r3, after0, after1, out):
    del after0, after1
    blocks = by_partner((r0, r1, r2, r3), ENTRY)
    lane = iota((256, LANES), 1)
    mask = same_sequence((256, 256))
    partials = []
    for left, right in ((0, 1), (2, 3)):
        first = second = None
        for part in (0, 1):
            x = row_group(blocks, left, part)
            y = row_group(blocks, right, part)
            zero = jnp.zeros_like(x)
            f = nt(jnp.where(lane < HEAD, x, zero), y)
            s = nt(jnp.where(lane < HEAD, zero, x), y)
            first = f if first is None else first + f
            second = s if second is None else second + s
        third = nt(row_group(blocks, left, 2), row_group(blocks, right, 2))
        for g in (first, second, third):
            g = jnp.where(mask, g, 0.0)
            partials.append(g.reshape(4, 8, 8, 256).sum(axis=1).reshape(32, 256))
    total = jnp.zeros((32, LANES), F32)
    row = iota((256, LANES), 0)
    column = ((row >> 6) << 2) + (row & 3)
    for k, t in enumerate(partials):
        place = (iota((256, LANES), 1) == column + 16 * k).astype(BF16)
        for _ in range(3):
            high = t.astype(BF16)
            total = total + nn(high, place)
            t = t - high.astype(F32)
    halves = [total[8 * d : 8 * d + 4] + total[8 * d + 4 : 8 * d + 8] for d in range(4)]
    out[...] = jnp.concatenate(halves, axis=0)


def row_grad_kernel(row_scale, p2, p3, p1, p0, b2, b3, b1, b0, after, *outs):
    del after
    outs[4][...] = jnp.zeros_like(outs[4])
    blocks = (b0, b1, b2, b3)
    total = (p0[...] + p1[...]) + (p2[...] + p3[...])
    dscores, weights = [], []
    for h in range(3):
        scores = total[:, 16 * h : 16 * h + 16] * row_scale
        dprob = total[:, 48 + 16 * h : 64 + 16 * h]
        e = jnp.exp(scores - jnp.max(scores, axis=1, keepdims=True))
        probs = e / jnp.sum(e, axis=1, keepdims=True)
        delta = jnp.sum(probs * dprob, axis=1, keepdims=True)
        dscores.append((probs * (dprob - delta) * row_scale).astype(BF16))
        weights.append(probs.astype(BF16))
    row = iota((256, 16), 0)
    spread = (iota((256, 16), 1) == ((row >> 6) << 2) + (row & 3)).astype(BF16)
    shape = (256, 256)
    mask = ((iota(shape, 0) >> 2) & 15) == ((iota(shape, 1) >> 2) & 15)
    keep = first_head(shape)
    plain = nn(spread, jnp.concatenate(dscores, axis=1)).astype(BF16)
    turned = nt(spread, jnp.concatenate(dscores + weights, axis=0)).astype(BF16)
    for k, array in enumerate((1, 0, 2)):
        mats = []
        for h in range(3):
            half = plain[:, 16 * h : 16 * h + 16] if k == 0 else turned[:, 48 * k - 48 + 16 * h : 48 * k - 32 + 16 * h]
            mats.append(jnp.where(mask, nt(half, spread), 0.0).astype(BF16))
        x = pair_rows(blocks, array)
        y = jnp.where(keep, nn(mats[0], x), nn(mats[1], x)).astype(BF16)
        z = nn(mats[2], single_rows(blocks, array)).astype(BF16)
        for n in range(4):
            outs[n][k * 128 : k * 128 + 64, :] = y[n * 64 : (n + 1) * 64, :LANES]
            outs[n][k * 128 + 64 : k * 128 + 128, :] = y[n * 64 : (n + 1) * 64, LANES:]
            outs[n][384 + k * 64 : 448 + k * 64, :] = z[n * 64 : (n + 1) * 64, :]


def reorder(rows, inner):
    bits = {16: 4, 32: 5}[inner]
    r = iota((rows, rows), 0)
    c = iota((rows, rows), 1)
    group = 4 * inner - 1
    source = (r & ~group) + ((r & (inner - 1)) << 2) + ((r & group) >> bits)
    return (c == source).astype(BF16)


def restore(rows, inner):
    bits = {16: 4, 32: 5}[inner]
    r = iota((rows, rows), 0)
    c = iota((rows, rows), 1)
    group = 4 * inner - 1
    source = (c & ~group) + ((c & (inner - 1)) << 2) + ((c & group) >> bits)
    return (r == source).astype(BF16)


def column_core_pair(col_scale, query, key, value, grad):
    heads = key.shape[0] // 128
    shape = (heads, 128, 128)
    scores = (nt(key, query) * col_scale).reshape(shape)
    dprob = nt(value, grad).reshape(shape)
    e = jnp.exp(scores - jnp.max(scores, axis=1, keepdims=True))
    probs = e * (1.0 / jnp.sum(e, axis=1, keepdims=True))
    delta = jnp.sum(probs * dprob, axis=1, keepdims=True)
    dscore = (probs * (dprob - delta) * col_scale).astype(BF16).reshape(heads * 128, 128)
    weights = probs.astype(BF16).reshape(heads * 128, 128)
    return tn(dscore, key), nn(dscore, query), nn(weights, grad)


def both(x):
    lane = iota(x.shape, 1)
    zero = jnp.zeros_like(x)
    return jnp.concatenate([jnp.where(lane < HEAD, x, zero), jnp.where(lane < HEAD, zero, x)], axis=0)


def column_grads(col_scale, columns, work, grads):
    lane = iota((128, LANES), 1)
    for c in columns:
        x = []
        for a in range(4):
            start = a * 128 + c * 32
            x.append(jnp.concatenate([work[d, start : start + 32, :] for d in range(4)], axis=0))
        query, key, grad, value = x
        dquery, dkey, dvalue = column_core_pair(col_scale, query, both(key), both(value), grad)
        dkey = jnp.where(lane < HEAD, dkey[:128], dkey[128:])
        dvalue = jnp.where(lane < HEAD, dvalue[:128], dvalue[128:])
        for k, y in enumerate((dquery, dkey, dvalue)):
            y = y.astype(BF16)
            for d in range(4):
                grads[d, k * 128 + c * 32 : k * 128 + (c + 1) * 32, :] = y[d * 32 : (d + 1) * 32, :]
        x = []
        for a in range(4):
            start = 512 + a * 64 + c * 16
            y = jnp.concatenate([work[d, start : start + 16, :] for d in range(4)], axis=0)
            x.append(jnp.concatenate([y[:, :HEAD], y[:, HEAD:]], axis=0))
        query, key, grad, value = x
        for k, y in enumerate(column_core_pair(col_scale, query, key, value, grad)):
            y = jnp.concatenate([y[:64], y[64:]], axis=1).astype(BF16)
            for d in range(4):
                start = 384 + k * 64 + c * 16
                grads[d, start : start + 16, :] = y[d * 16 : (d + 1) * 16, :]


def column_first_kernel(col_scale, b2, b3, b1, b0, after, work, grads):
    del after
    blocks = (b0, b1, b2, b3)
    pair_order, single_order = reorder(128, 32), reorder(128, 16)
    for d in range(4):
        x = [blocks[d][a * 128 : (a + 1) * 128, :] for a in range(6)]
        for a in (0, 2):
            y = nn(pair_order, jnp.concatenate([x[a], x[a + 1]], axis=1)).astype(BF16)
            work[d, a * 128 : (a + 1) * 128, :] = y[:, :LANES]
            work[d, (a + 1) * 128 : (a + 2) * 128, :] = y[:, LANES:]
        y = nn(single_order, jnp.concatenate([x[4], x[5]], axis=1)).astype(BF16)
        work[d, 512:640, :] = y[:, :LANES]
        work[d, 640:768, :] = y[:, LANES:]
    column_grads(col_scale, FIRST_COLUMNS, work, grads)


def joined(first, second, d, start, size, split):
    middle, stop = start + split * size, start + 4 * size
    return jnp.concatenate([first[d, start:middle, :], second[d, middle:stop, :]], axis=0)


def column_second_kernel(col_scale, work, first, after, o0, o1, o2, o3, grads):
    del after
    outs = (o0, o1, o2, o3)
    column_grads(col_scale, SECOND_COLUMNS, work, grads)
    split = len(FIRST_COLUMNS)
    pair_back, single_back = restore(128, 32), restore(64, 16)
    for d in range(4):
        x = [joined(first, grads, d, k * 128, 32, split) for k in range(3)]
        y = nn(pair_back, jnp.concatenate(x, axis=1)).astype(BF16)
        for k in range(3):
            outs[d][k * 128 : (k + 1) * 128, :] = y[:, k * LANES : (k + 1) * LANES]
        x = [joined(first, grads, d, 384 + k * 64, 16, split) for k in range(3)]
        y = nn(single_back, jnp.concatenate(x, axis=1)).astype(BF16)
        for k in range(3):
            outs[d][384 + k * 64 : 448 + k * 64, :] = y[:, k * LANES : (k + 1) * LANES]


def tick_kernel(*refs):
    refs[-1][...] = jnp.zeros_like(refs[-1])


VMEM = pl.BlockSpec(memory_space=pltpu.VMEM)
ANY = pl.BlockSpec(memory_space=pl.ANY)
HBM = pl.BlockSpec(memory_space=pltpu.HBM)
LIMIT = 40 * 1024 * 1024
ROW = 1
TICK = 20_000_000_000
CHUNKS = 2
FIRST_COLUMNS = (0,)
SECOND_COLUMNS = (1, 2, 3)
COL = 4_000_000_000
ENTRY = (2, 1, 3, 0)
RETURN = (1, 3, 2, 0)
SHIFTS = (2, 3, 1)


def call(body, shapes, operands, name, flops, scratch=(), in_space=VMEM, out_space=VMEM):
    kernel = pl.pallas_call(
        body,
        out_shape=[jax.ShapeDtypeStruct(shape, dtype) for shape, dtype in shapes],
        in_specs=in_space if isinstance(in_space, list) else [in_space] * len(operands),
        out_specs=[out_space] * len(shapes),
        scratch_shapes=list(scratch),
        compiler_params=pltpu.CompilerParams(vmem_limit_bytes=LIMIT),
        cost_estimate=pl.CostEstimate(flops=flops, bytes_accessed=1, transcendentals=0),
        name=name,
    )
    return list(kernel(*operands))


def far_first(blocks):
    return [blocks[2], blocks[3], blocks[1], blocks[0]]


def near_first(blocks):
    return [blocks[1], blocks[2], blocks[3], blocks[0]]


def exchange(blocks, axis, shifts=SHIFTS):
    moved = list(blocks)
    for d in shifts:
        moved[d] = lax.ppermute(blocks[d], axis, [(i, i ^ d) for i in range(4)])
    return moved


def pack(arrays, axis, name):
    arrays = [pltpu.with_memory_space_constraint(x, pltpu.HBM) for x in arrays]
    scratch = (pltpu.VMEM((4, *arrays[0].shape), BF16), pltpu.SemaphoreType.DMA((4 * CHUNKS,)))
    shapes = [((192, 4, LANES), BF16)] * 4
    blocks = call(functools.partial(pack_kernel, axis), shapes, arrays, name, 1, scratch, in_space=HBM)
    return [b.reshape(768, LANES) for b in blocks]


def tick(operands, name, flops):
    return call(tick_kernel, [((8, LANES), F32)], operands, name, flops, in_space=ANY)


def unpack(row_back, col_back, after, shape):
    operands = [b.reshape(144, 4, LANES) for b in [row_back[d] for d in RETURN] + far_first(col_back)]
    operands += after
    scratch = (pltpu.VMEM((6, *shape), BF16), pltpu.SemaphoreType.DMA((6 * CHUNKS,)))
    return call(unpack_kernel, [(shape, BF16)] * 6, operands, "unpack", 1, scratch, out_space=HBM)


def local_fast(row_query, row_key, row_value, row_grad, col_query, col_key, col_value, col_grad):
    shape = row_query.shape
    seqs = shape[0] * lax.axis_size("seq")
    row_scale = HEAD ** (-0.5) * seqs ** (-0.5)
    col_scale = HEAD ** (-0.5)
    row_blocks = pack((row_query, row_key, row_grad, row_value), "col", "row_pack")
    row_blocks = exchange(row_blocks, "col")
    col_blocks = pack((col_query, col_key, col_grad, col_value), "seq", "col_pack")
    col_blocks = exchange(col_blocks, "seq")
    (part,) = call(row_score_kernel, [((16, LANES), F32)], [row_blocks[d] for d in ENTRY] + far_first(col_blocks)[:2], "row_scores", ROW)
    parts = exchange([part] * 4, "seq")
    col_work, col_first = call(
        functools.partial(column_first_kernel, col_scale),
        [((4, 768, LANES), BF16), ((4, 576, LANES), BF16)],
        [*far_first(col_blocks), part],
        "col_grads_first",
        COL,
    )
    *row_out, token = call(
        functools.partial(row_grad_kernel, row_scale),
        [((576, LANES), BF16)] * 4 + [((8, LANES), F32)],
        far_first(parts) + far_first(row_blocks) + [col_first],
        "row_grads",
        ROW,
    )
    row_back = exchange(row_out, "col", (1, 2, 3))
    col_out = call(
        functools.partial(column_second_kernel, col_scale),
        [((576, LANES), BF16)] * 4,
        [col_work, col_first, token],
        "col_grads_second",
        COL,
        scratch=(pltpu.VMEM((4, 576, LANES), BF16),),
    )
    col_back = exchange(col_out, "seq")
    arrived = tick(far_first(row_back)[:3], "row_arrived", TICK)
    return tuple(unpack(row_back, col_back, arrived, shape))


def tied_terms(scores, prob_grad, row_scale):
    row_probs = jax.nn.softmax(scores, axis=-1)
    row_delta = jnp.sum(row_probs * prob_grad, axis=-1, keepdims=True)
    score_gradient_part = row_probs * (prob_grad - row_delta) * row_scale
    return (row_probs.astype(BF16), score_gradient_part.astype(BF16))


def einsum(spec, a, b):
    return jnp.einsum(spec, a, b, preferred_element_type=F32)


def column_core(query, key, value, grad, col_scale):
    scores = einsum("qzd,izd->zqi", query, key) * col_scale
    prob_grad = einsum("qzd,izd->zqi", grad, value)
    weights, dscore = tied_terms(scores, prob_grad, col_scale)
    return (
        einsum("zqi,izd->qzd", dscore, key).astype(BF16),
        einsum("zqi,qzd->izd", dscore, query).astype(BF16),
        einsum("zqi,qzd->izd", weights, grad).astype(BF16),
    )


def local_general(row_query, row_key, row_value, row_grad, col_query, col_key, col_value, col_grad):
    seq_dev, col_dev, width = row_query.shape
    seqs = seq_dev * lax.axis_size("seq")
    cols = col_dev * lax.axis_size("col")
    row_scale = HEAD ** (-0.5) * seqs ** (-0.5)
    col_scale = HEAD ** (-0.5)
    moved = [
        lax.all_to_all(x, "col", split_axis=0, concat_axis=1, tiled=True)
        for x in (row_query, row_key, row_value, row_grad)
    ]
    own_rows = moved[0].shape[0]
    query, key, value, grad = (x.reshape(own_rows, cols, HEADS, HEAD) for x in moved)
    score_part = einsum("sihe,sjhe->hij", query, key) * row_scale
    prob_part = einsum("sihe,sjhe->hij", grad, value)
    scores, prob_grad = lax.psum((score_part, prob_part), ("col", "seq"))
    weights, dscore = tied_terms(scores, prob_grad, row_scale)
    row_back = [
        lax.all_to_all(
            y.astype(BF16).reshape(own_rows, cols, width), "col", split_axis=1, concat_axis=0, tiled=True
        )
        for y in (
            einsum("hij,sjhe->sihe", dscore, key),
            einsum("hij,sihe->sjhe", dscore, query),
            einsum("hij,sihe->sjhe", weights, grad),
        )
    ]
    col_moved = [
        lax.all_to_all(
            x.reshape(seq_dev, col_dev * width), "seq", split_axis=1, concat_axis=0, tiled=True
        )
        for x in (col_query, col_key, col_value, col_grad)
    ]
    share = col_moved[0].shape[1]
    col_grads = column_core(*(x.reshape(seqs, share // HEAD, HEAD) for x in col_moved), col_scale)
    col_back = [
        lax.all_to_all(y.reshape(seqs, share), "seq", split_axis=0, concat_axis=1, tiled=True)
        for y in col_grads
    ]
    return (*row_back, *(y.reshape(seq_dev, col_dev, width) for y in col_back))


def local(*arrays):
    sizes = (lax.axis_size("col"), lax.axis_size("seq"))
    if sizes == (4, 4) and arrays[0].shape == (32, 4, HEADS * HEAD):
        return local_fast(*arrays)
    return local_general(*arrays)


def solution(mesh):
    spec = P(("grp", "seq"), "col", None)
    return jax.shard_map(
        local, mesh=mesh, in_specs=(spec,) * 8, out_specs=(spec,) * 6, check_vma=False
    )
```
